128 devices in a mesh: section: 4 (over z), dp: 32 (over x, y, core).
Axes of the slice: x: 4, y: 4, z: 4, core: 2. Of those that a mesh axis runs over, the one named last changes fastest.
Arguments:
- saved_inputs: bfloat16 [4, 32, 4, 48, 4096], P('section', 'dp'), may hold values from -6 to 6
- cotangent: bfloat16 [32, 4, 48, 4096], P('dp'), may hold values from -6 to 6
- out_proj: bfloat16 [4, 2048, 4096], P('section'), may hold values from -1 to 1
- norm_gain: float32 [4, 2048], P('section'), may hold values from 0.5 to 1.5
- lengths: int32 [32, 4], P('dp'), may hold values from 6 to 48, as said below
Outputs:
- input_grad: bfloat16 [4, 32, 4, 48, 4096], P('section', 'dp')
- proj_grad: float32 [4, 2048, 4096], P('section', 'dp')
- gain_grad: float32 [4, 2048], P('section', 'dp')
The draws below stay inside these ranges and needn't reach their ends.
Inputs may be any that keep to these rules, and one draw needn't show every extreme that they name: `lengths`: every replica's micro-batch has at least 2 live cells; some micro-batch has exactly 48.
All inputs are finite; a program needn't handle non-finite values.
Results may differ from the reference program's by a relative error of at most 0.03.
Values may be sent and summed in bfloat16 or wider, within the bound.
No kernel may reach another device: no remote copies, remote signals or barrier semaphores. Data moves between devices by JAX's collectives and lax.ppermute only.
A program may use at most 192 MiB of HBM per device.

```python
import math
import jax
import jax.numpy as jnp
from jax import lax

D = 4096
HEAD = 128
HW = 2048
MB = 4
LMAX = 48
SECTIONS = 4
REPLICAS = 32
N_SECTION = 4


def draw_lengths(key, part):
    lowest = max(2, LMAX // 8)
    values = jax.random.randint(key, (REPLICAS * MB,), lowest, LMAX + 1)
    chosen = jax.random.randint(jax.random.fold_in(key, 7), (), 0, REPLICAS * MB)
    values = values.at[chosen].set(LMAX)
    return values.reshape(REPLICAS, MB).astype(jnp.int32)


def section_base(key, section_pos):
    field_shape = (REPLICAS, MB, LMAX, D)
    common_key = jax.random.fold_in(key, 11)
    own_key = jax.random.fold_in(jax.random.fold_in(key, 13), section_pos)
    common = jax.random.normal(common_key, field_shape, jnp.float32)
    own = jax.random.normal(own_key, field_shape, jnp.float32)
    return common + 0.4 * own


def draw_saved_inputs(key, part):
    stacked = []
    for section_pos in range(SECTIONS):
        field = section_base(key, section_pos)
        field = jnp.clip(field, -6.0, 6.0)
        stacked.append(field)
    return jnp.stack(stacked).astype(jnp.bfloat16)


def draw_cotangent(key, part):
    field = section_base(key, SECTIONS - 1)
    noise_key = jax.random.fold_in(key, 17)
    field_shape = (REPLICAS, MB, LMAX, D)
    noise = jax.random.normal(noise_key, field_shape, jnp.float32)
    return jnp.clip(field + 0.6 * noise, -6.0, 6.0).astype(jnp.bfloat16)


def draw_out_proj(key, part):
    noise_key = jax.random.fold_in(key, 23)
    full_shape = (SECTIONS, HW, D)
    noise = jnp.clip(jax.random.normal(noise_key, full_shape, jnp.float32), -6.0, 6.0)
    noise = noise * HW ** (-0.5)
    diagonal = (jnp.arange(HW)[:, None] == jnp.arange(D)[None, :]).astype(jnp.float32)
    return jnp.clip(noise + diagonal[None], -1.0, 1.0).astype(jnp.bfloat16)


def setup_inputs(seed: int = 0) -> dict:
    arg_keys = jax.random.split(jax.random.key(seed), 6)
    saved_inputs = draw_saved_inputs(jax.random.fold_in(arg_keys[5], 71), 0)
    cotangent = draw_cotangent(jax.random.fold_in(arg_keys[5], 71), 0)
    out_proj = draw_out_proj(jax.random.fold_in(arg_keys[5], 71), 0)
    norm_gain = jnp.clip(1.0 + 0.1 * jax.random.normal(arg_keys[3], (SECTIONS, HW), jnp.float32), 0.5, 1.5)
    lengths = draw_lengths(jax.random.fold_in(arg_keys[5], 71), 0)
    return {"saved_inputs": saved_inputs, "cotangent": cotangent, "out_proj": out_proj, "norm_gain": norm_gain, "lengths": lengths}


norm_eps = 1e-06
score_factor = 0.6
masked_score = -1e+30

def lowered(values):
    return lax.optimization_barrier(values.astype(jnp.bfloat16))

def layer_grad(activations, upstream, length, weight, gain_row):
    row_count = activations.shape[0]
    full_width = activations.shape[1]
    hidden = weight.shape[0]
    head_count = hidden // HEAD
    score_scale = score_factor / math.sqrt(HEAD)
    act_float = activations.astype(jnp.float32)
    inv_rms = lax.rsqrt(lax.optimization_barrier(jnp.mean(act_float * act_float, axis=1, keepdims=True)) + norm_eps)
    normed = act_float[:, :hidden] * inv_rms
    shared = lowered(normed * gain_row)
    live_rows = jnp.arange(row_count) < length
    heads_view = shared.astype(jnp.float32).reshape(row_count, head_count, HEAD)
    scores = jnp.einsum('ihd,jhd->hij', heads_view, heads_view) * score_scale
    scores = jnp.where(live_rows[None, None, :], scores, masked_score)
    scores = scores - lax.optimization_barrier(jnp.max(scores, axis=2, keepdims=True))
    exponent = jnp.exp(scores)
    attention = exponent / lax.optimization_barrier(jnp.sum(exponent, axis=2, keepdims=True))
    attn_low = lowered(attention).astype(jnp.float32)
    attended = jnp.einsum('hij,jhd->ihd', attn_low, heads_view).reshape(row_count, hidden).astype(jnp.bfloat16)
    masked = jnp.where(live_rows[:, None], upstream, jnp.zeros_like(upstream))
    grad_attn = lowered(jnp.dot(masked, weight.T, preferred_element_type=jnp.float32))
    grad_heads = grad_attn.astype(jnp.float32).reshape(row_count, head_count, HEAD)
    grad_probs = jnp.einsum('ihd,jhd->hij', grad_heads, heads_view)
    row_delta = lax.optimization_barrier(jnp.sum(attention * grad_probs, axis=2, keepdims=True))
    dscore = lowered(score_scale * attention * (grad_probs - row_delta)).astype(jnp.float32)
    grad_shared = jnp.einsum('hij,jhd->ihd', dscore, heads_view)
    grad_shared = grad_shared + jnp.einsum('hij,ihd->jhd', dscore, heads_view)
    grad_shared = grad_shared + jnp.einsum('hij,ihd->jhd', attn_low, grad_heads)
    grad_shared = grad_shared.reshape(row_count, hidden)
    gain_term = lax.optimization_barrier(jnp.sum(grad_shared * normed, axis=0))
    scaled = grad_shared * gain_row
    inner_sum = lax.optimization_barrier(jnp.sum(scaled * act_float[:, :hidden], axis=1, keepdims=True))
    direct = jnp.concatenate([inv_rms * scaled, jnp.zeros((row_count, full_width - hidden), jnp.float32)], axis=1)
    result = upstream.astype(jnp.float32) + direct - act_float * inv_rms ** 3 * inner_sum / full_width
    return (result.astype(jnp.bfloat16), attended, masked, gain_term)

def reference(saved_inputs, cotangent, out_proj, norm_gain, lengths):
    upstream_all = cotangent
    grad_list = [None] * N_SECTION
    proj_list = [None] * N_SECTION
    gain_list = [None] * N_SECTION
    for section_pos in range(N_SECTION - 1, -1, -1):
        weight = out_proj[section_pos]
        gain_row = norm_gain[section_pos]

        def replica_step(totals, operand_set):
            inputs, upstream, length_table = operand_set
            replica_w = jnp.zeros((HW, D), jnp.float32)
            replica_g = jnp.zeros((HW,), jnp.float32)
            collected = []
            for micro_pos in range(MB):
                grad_out, attended, masked, gain_term = layer_grad(inputs[micro_pos], upstream[micro_pos], length_table[micro_pos], weight, gain_row)
                replica_w = replica_w + jnp.dot(attended.T, masked, preferred_element_type=jnp.float32)
                replica_g = replica_g + gain_term
                collected.append(grad_out)
            total_w, total_g = totals
            total_w = total_w + lowered(replica_w).astype(jnp.float32)
            total_g = total_g + lowered(replica_g).astype(jnp.float32)
            return ((total_w, total_g), jnp.stack(collected))
        start_totals = (jnp.zeros((HW, D), jnp.float32), jnp.zeros((HW,), jnp.float32))
        (total_w, total_g), grad_store = lax.scan(replica_step, start_totals, (saved_inputs[section_pos], upstream_all, lengths))
        grad_list[section_pos] = grad_store
        proj_list[section_pos] = total_w
        gain_list[section_pos] = total_g
        upstream_all = grad_store
    return (jnp.stack(grad_list), jnp.stack(proj_list), jnp.stack(gain_list))
```

```python
import math

import jax
import jax.numpy as jnp
from jax import lax
from jax.experimental import pallas as pl
from jax.experimental.pallas import tpu as pltpu
from jax.sharding import Mesh
from jax.sharding import PartitionSpec as P

HEAD = 128
NORM_EPS = 1e-06
SCORE_FACTOR = 0.6
MASKED_SCORE = -1e30
DP = "dp"
SKEW = 2


def dot_nt(a, b):
    return lax.dot_general(a, b, (((1,), (1,)), ((), ())), preferred_element_type=jnp.float32)


def dot_nn(a, b):
    return lax.dot_general(a, b, (((1,), (0,)), ((), ())), preferred_element_type=jnp.float32)


def dot_tn(a, b):
    return lax.dot_general(a, b, (((0,), (0,)), ((), ())), preferred_element_type=jnp.float32)


def prelude_body(heads, lengths, x_ref, gain_ref, shared_ref, probs_ref, attended_ref, inv_ref, *, micro):
    scale = SCORE_FACTOR / math.sqrt(HEAD)
    rows = x_ref.shape[0]
    hidden = shared_ref.shape[1]
    x = x_ref[...].astype(jnp.float32)
    inv = lax.rsqrt(jnp.mean(x * x, axis=1, keepdims=True) + NORM_EPS)
    inv_ref[...] = jnp.broadcast_to(inv, inv_ref.shape)
    shared_ref[...] = (x[:, :hidden] * inv * gain_ref[...]).astype(jnp.bfloat16)
    live = lax.broadcasted_iota(jnp.int32, (rows, rows), 1) < lengths[micro]
    for head in range(heads):
        cols = slice(head * HEAD, (head + 1) * HEAD)
        shared = shared_ref[:, cols]
        scores = jnp.where(live, dot_nt(shared, shared) * scale, MASKED_SCORE)
        exponent = jnp.exp(scores - jnp.max(scores, axis=1, keepdims=True))
        probs = exponent / jnp.sum(exponent, axis=1, keepdims=True)
        probs_ref[head] = probs
        attended_ref[:, cols] = dot_nn(probs.astype(jnp.bfloat16), shared).astype(jnp.bfloat16)


def prelude(micro, lengths, inputs, gain_row):
    micros, rows, width = inputs.shape
    hidden = gain_row.shape[1]
    heads = hidden // HEAD

    def body(lengths_ref, *refs):
        prelude_body(heads, lengths_ref, *refs, micro=micro)

    return pl.pallas_call(
        body,
        name="prelude",
        grid_spec=pltpu.PrefetchScalarGridSpec(
            num_scalar_prefetch=1,
            grid=(1,),
            in_specs=[
                pl.BlockSpec((None, rows, width), lambda i, n: (micro, 0, 0)),
                pl.BlockSpec((1, hidden), lambda i, n: (0, 0)),
            ],
            out_specs=[
                pl.BlockSpec((rows, hidden), lambda i, n: (0, 0)),
                pl.BlockSpec((heads, rows, rows), lambda i, n: (0, 0, 0)),
                pl.BlockSpec((rows, hidden), lambda i, n: (0, 0)),
                pl.BlockSpec((rows, HEAD), lambda i, n: (0, 0)),
            ],
        ),
        out_shape=[
            jax.ShapeDtypeStruct((rows, hidden), jnp.bfloat16),
            jax.ShapeDtypeStruct((heads, rows, rows), jnp.float32),
            jax.ShapeDtypeStruct((rows, hidden), jnp.bfloat16),
            jax.ShapeDtypeStruct((rows, HEAD), jnp.float32),
        ],
        compiler_params=pltpu.CompilerParams(vmem_limit_bytes=16 << 20),
        cost_estimate=pl.CostEstimate(flops=40_000_000, bytes_accessed=2_000_000, transcendentals=40_000),
    )(lengths, inputs, gain_row)


def layer_body(
    flags, weight_ref, x_ref, shared_ref, probs_ref, inv_ref, gain_ref, gacc_ref, cot_ref, inc_ref,
    store_in, masked_in, out_ref, gout_ref, store_ref, masked_ref,
    raw, live, tiles, scaled_ref, inner_ref, sems, *, heads_step, width,
):
    step = pl.program_id(0)
    steps = pl.num_programs(0)
    micro = flags[1]
    scale = SCORE_FACTOR / math.sqrt(HEAD)
    rows = raw.shape[0]
    hidden = shared_ref.shape[1]
    active = flags[0] == 1
    tile_copy = pltpu.make_async_copy(tiles, masked_ref.at[:, micro], sems.at[1])

    @pl.when(jnp.logical_and(step == 0, jnp.logical_not(active)))
    def _():
        gout_ref[...] = gacc_ref[...]

    @pl.when(jnp.logical_and(step == 0, active))
    def _():
        @pl.when(flags[3] == 1)
        def _():
            copy = pltpu.make_async_copy(cot_ref.at[micro], raw, sems.at[0])
            copy.start()
            copy.wait()

        @pl.when(flags[3] == 0)
        def _():
            copy = pltpu.make_async_copy(inc_ref, raw, sems.at[0])
            copy.start()
            copy.wait()

        keep = lax.broadcasted_iota(jnp.int32, (rows, width), 0) < flags[2]
        upstream = raw[...]
        live[...] = jnp.where(keep, upstream.astype(jnp.float32), 0.0).astype(jnp.bfloat16)
        for tile in range(width // HEAD):
            tiles[tile] = live[:, tile * HEAD : (tile + 1) * HEAD]
        tile_copy.start()
        inner_ref[...] = jnp.zeros_like(inner_ref)

    @pl.when(active)
    def _():
        wide = heads_step * HEAD
        base = pl.multiple_of(step * wide, wide)
        grad_attn = dot_nt(live[...], weight_ref[...]).astype(jnp.bfloat16)
        inv = inv_ref[...]
        inner = inner_ref[...]
        for local in range(heads_step):
            cols = pl.ds(pl.multiple_of(base + local * HEAD, HEAD), HEAD)
            shared = shared_ref[:, cols]
            probs = probs_ref[step * heads_step + local]
            grad_head = grad_attn[:, local * HEAD : (local + 1) * HEAD]
            grad_probs = dot_nt(grad_head, shared)
            delta = jnp.sum(probs * grad_probs, axis=1, keepdims=True)
            dscore = scale * probs * (grad_probs - delta)
            low = dscore.astype(jnp.bfloat16)
            low_t = dscore.T.astype(jnp.bfloat16)
            probs_t = probs.T.astype(jnp.bfloat16)
            grad_shared = dot_nn(low, shared) + dot_nn(low_t, shared) + dot_nn(probs_t, grad_head)
            x_head = x_ref[:, cols].astype(jnp.float32)
            gout_ref[:, cols] = gacc_ref[:, cols] + jnp.sum(grad_shared * (x_head * inv), axis=0, keepdims=True)
            scaled = grad_shared * gain_ref[:, cols]
            inner = inner + scaled * x_head
            scaled_ref[:, cols] = scaled
        inner_ref[...] = inner

    @pl.when(jnp.logical_and(step == steps - 1, active))
    def _():
        inv = inv_ref[:, :1]
        coef = inv * inv * inv * (jnp.sum(inner_ref[...], axis=1, keepdims=True) / width)
        low = raw[:, :hidden].astype(jnp.float32) + inv * scaled_ref[...] - x_ref[:, :hidden].astype(jnp.float32) * coef
        out_ref[:, :hidden] = low.astype(jnp.bfloat16)
        high = raw[:, hidden:].astype(jnp.float32) - x_ref[:, hidden:].astype(jnp.float32) * coef
        out_ref[:, hidden:] = high.astype(jnp.bfloat16)
        copy = pltpu.make_async_copy(out_ref, store_ref.at[micro], sems.at[2])
        copy.start()
        tile_copy.wait()
        copy.wait()


def layer_step(flags, weight, inputs, shared, probs, inv, gain_row, gain_acc, cotangent, incoming, store, masked):
    micros, rows, width = inputs.shape
    hidden = weight.shape[0]
    heads = hidden // HEAD
    heads_step = 2
    steps = heads // heads_step

    def body(*refs):
        layer_body(*refs, heads_step=heads_step, width=width)

    anywhere = pl.BlockSpec(memory_space=pl.ANY)
    return pl.pallas_call(
        body,
        name="layer_step",
        grid_spec=pltpu.PrefetchScalarGridSpec(
            num_scalar_prefetch=1,
            grid=(steps,),
            in_specs=[
                pl.BlockSpec((heads_step * HEAD, width), lambda i, f: (i * f[0], 0)),
                pl.BlockSpec((None, rows, width), lambda i, f: (f[1], 0, 0)),
                pl.BlockSpec((None, rows, hidden), lambda i, f: (f[1], 0, 0)),
                pl.BlockSpec((None, heads, rows, rows), lambda i, f: (f[1], 0, 0, 0)),
                pl.BlockSpec((None, rows, HEAD), lambda i, f: (f[1], 0, 0)),
                pl.BlockSpec((1, hidden), lambda i, f: (0, 0)),
                pl.BlockSpec((1, hidden), lambda i, f: (0, 0)),
                anywhere,
                anywhere,
                anywhere,
                anywhere,
            ],
            out_specs=[
                pl.BlockSpec((rows, width), lambda i, f: (0, 0)),
                pl.BlockSpec((1, hidden), lambda i, f: (0, 0)),
                anywhere,
                anywhere,
            ],
            scratch_shapes=[
                pltpu.VMEM((rows, width), jnp.bfloat16),
                pltpu.VMEM((rows, width), jnp.bfloat16),
                pltpu.VMEM((width // HEAD, rows, HEAD), jnp.bfloat16),
                pltpu.VMEM((rows, hidden), jnp.float32),
                pltpu.VMEM((rows, HEAD), jnp.float32),
                pltpu.SemaphoreType.DMA((3,)),
            ],
        ),
        out_shape=[
            jax.ShapeDtypeStruct((rows, width), jnp.bfloat16),
            jax.ShapeDtypeStruct((1, hidden), jnp.float32),
            jax.ShapeDtypeStruct(store.shape, store.dtype),
            jax.ShapeDtypeStruct(masked.shape, masked.dtype),
        ],
        input_output_aliases={10: 2, 11: 3},
        compiler_params=pltpu.CompilerParams(vmem_limit_bytes=24 << 20),
        cost_estimate=pl.CostEstimate(flops=850_000_000, bytes_accessed=19_000_000, transcendentals=0),
    )(flags, weight, inputs, shared, probs, inv, gain_row, gain_acc, cotangent, incoming, store, masked)


def scratch_buffers(shapes):
    def body(*refs):
        pass

    return pl.pallas_call(
        body,
        name="buffers",
        out_specs=[pl.BlockSpec(memory_space=pl.ANY)] * len(shapes),
        out_shape=[jax.ShapeDtypeStruct(shape, dtype) for shape, dtype in shapes],
    )()


def per_device(saved_inputs, cotangent, out_proj, norm_gain, lengths):
    sections = lax.axis_size("section")
    section = lax.axis_index("section")
    replicas = lax.axis_size(DP)
    weight = out_proj[0]
    gain_row = norm_gain
    inputs = saved_inputs[0, 0]
    upstream = cotangent[0]
    table = lengths[0]
    micros, rows, width = inputs.shape
    hidden = weight.shape[0]
    tiles = width // HEAD

    store, masked = scratch_buffers(
        [((micros, rows, width), jnp.bfloat16), ((tiles, micros, rows, HEAD), jnp.bfloat16)]
    )
    gain_acc = jnp.zeros((1, hidden), jnp.float32)
    pre = [prelude(micro, table, inputs, gain_row) for micro in range(micros)]
    shared, probs, attended, inv = (jnp.stack(parts) for parts in zip(*pre))
    attended_all = lax.all_gather(attended.reshape(micros * rows, hidden), DP, axis=0, tiled=True)

    steps = SKEW * (sections - 1) + micros
    at_top = (section == sections - 1).astype(jnp.int32)
    arriving = {}
    for step in range(steps):
        micro = step - SKEW * (sections - 1 - section)
        active = jnp.logical_and(micro >= 0, micro < micros).astype(jnp.int32)
        chosen = jnp.clip(micro, 0, micros - 1)
        flags = jnp.stack([active, chosen, table[chosen], at_top]).astype(jnp.int32)
        incoming = arriving.get(step)
        if incoming is None:
            incoming = upstream[0]
        grad_out, gain_acc, store, masked = layer_step(
            flags, weight, inputs, shared, probs, inv, gain_row, gain_acc, upstream, incoming, store, masked
        )
        route = [
            (src, src - 1)
            for src in range(1, sections)
            if 0 <= step - SKEW * (sections - 1 - src) < micros
        ]
        if route:
            arriving[step + SKEW] = lax.ppermute(grad_out, "section", route)

    columns = lax.all_to_all(masked.reshape(tiles, micros * rows, HEAD), DP, 0, 0, tiled=True)
    columns = columns.reshape(replicas * micros * rows, HEAD)
    summed = dot_tn(attended_all, columns).astype(jnp.bfloat16)
    own = hidden // replicas
    block = lax.all_to_all(summed.reshape(replicas, own, HEAD), DP, 0, 0, tiled=True)
    proj = block.transpose(1, 0, 2).reshape(own, width).astype(jnp.float32)
    gain_blocks = lax.all_to_all(
        gain_acc.reshape(replicas, 1, own), DP, 0, 0, tiled=True
    )
    gain = jnp.sum(gain_blocks.astype(jnp.bfloat16).astype(jnp.float32), axis=(0, 1))
    return (store[None, None], proj[None], gain[None])


def solution(mesh):
    placed = (
        P("section", "dp", None, None, None),
        P("dp", None, None, None),
        P("section", None, None),
        P("section", None),
        P("dp", None),
    )
    return jax.shard_map(
        per_device,
        mesh=mesh,
        in_specs=placed,
        out_specs=(
            P("section", "dp", None, None, None),
            P("section", "dp", None),
            P("section", "dp"),
        ),
        check_vma=False,
    )
```

```python
import math

import jax
import jax.numpy as jnp
from jax import lax
from jax.experimental import pallas as pl
from jax.experimental.pallas import tpu as pltpu
from jax.sharding import PartitionSpec as P

HEAD = 128
NORM_EPS = 1e-06
SCORE_FACTOR = 0.6
MASKED_SCORE = -1e30
DP = "dp"
SKEW = 2
CHUNK = 256
LIMIT = 8 << 20
PARTS = 3
DEPTH = 512
PAD = 80

VMEM = pl.BlockSpec(memory_space=pltpu.VMEM)
SMEM = pl.BlockSpec(memory_space=pltpu.SMEM)
FAR = pl.BlockSpec(memory_space=pl.ANY)


def dot_nt(a, b):
    return lax.dot_general(a, b, (((1,), (1,)), ((), ())), preferred_element_type=jnp.float32)


def dot_nn(a, b):
    return lax.dot_general(a, b, (((1,), (0,)), ((), ())), preferred_element_type=jnp.float32)


def dot_tn(a, b):
    return lax.dot_general(a, b, (((0,), (0,)), ((), ())), preferred_element_type=jnp.float32)


def prelude_body(lengths, x_far, gain_ref, weight_far, cot_far, weight_ref, x_ref, cot_ref, shared_ref, probs_ref,
                 turned_ref, inv_ref, early_ref, late_ref, sems):
    scale = SCORE_FACTOR / math.sqrt(HEAD)
    micros, rows, _ = x_ref.shape
    hidden = shared_ref.shape[2]
    loads = [
        pltpu.make_async_copy(x_far.at[micro], x_ref.at[micro], sems.at[micro]) for micro in range(micros)
    ]
    loads.append(pltpu.make_async_copy(cot_far, cot_ref, sems.at[micros]))
    loads.append(pltpu.make_async_copy(weight_far, weight_ref, sems.at[micros + 1]))
    for load in loads:
        load.start()
    for micro in range(micros):
        loads[micro].wait()
        x = x_ref[micro].astype(jnp.float32)
        inv = lax.rsqrt(jnp.mean(x * x, axis=1, keepdims=True) + NORM_EPS)
        inv_ref[micro] = jnp.broadcast_to(inv, (rows, HEAD))
        shared_ref[micro] = (x[:, :hidden] * inv * gain_ref[...]).astype(jnp.bfloat16)
        live = lax.broadcasted_iota(jnp.int32, (rows, rows), 1) < lengths[0, micro]
        half = micros // 2
        out = early_ref if micro < half else late_ref
        first = (micro % half) * rows
        for head in range(hidden // HEAD):
            cols = slice(head * HEAD, (head + 1) * HEAD)
            shared = shared_ref[micro, :, cols]
            scores = jnp.where(live, dot_nt(shared, shared) * scale, MASKED_SCORE)
            exponent = jnp.exp(scores - jnp.max(scores, axis=1, keepdims=True))
            probs = exponent / jnp.sum(exponent, axis=1, keepdims=True)
            probs_ref[micro, head] = probs
            turned_ref[micro, head] = probs.T.astype(jnp.bfloat16)
            out[first : first + rows, cols] = dot_nn(probs.astype(jnp.bfloat16), shared).astype(jnp.bfloat16)
    for load in loads[micros:]:
        load.wait()


def prelude(table, inputs, gain_row, weight, upstream):
    micros, rows, width = inputs.shape
    hidden = gain_row.shape[1]
    heads = hidden // HEAD
    half = jax.ShapeDtypeStruct((micros // 2 * rows, hidden), jnp.bfloat16)
    return pl.pallas_call(
        prelude_body,
        name="prelude",
        in_specs=[SMEM, FAR, VMEM, FAR, FAR],
        out_specs=[VMEM] * 9,
        out_shape=[
            jax.ShapeDtypeStruct(weight.shape, jnp.bfloat16),
            jax.ShapeDtypeStruct(inputs.shape, jnp.bfloat16),
            jax.ShapeDtypeStruct(inputs.shape, jnp.bfloat16),
            jax.ShapeDtypeStruct((micros, rows, hidden), jnp.bfloat16),
            jax.ShapeDtypeStruct((micros, heads, rows, rows), jnp.float32),
            jax.ShapeDtypeStruct((micros, heads, rows, rows), jnp.bfloat16),
            jax.ShapeDtypeStruct((micros, rows, HEAD), jnp.float32),
            half,
            half,
        ],
        scratch_shapes=[pltpu.SemaphoreType.DMA((micros + 2,))],
        compiler_params=pltpu.CompilerParams(vmem_limit_bytes=LIMIT),
        cost_estimate=pl.CostEstimate(flops=500_000_000, bytes_accessed=22_000_000, transcendentals=200_000),
    )(table, inputs, gain_row, weight, upstream)


def place(step, micros):
    above = lax.axis_size("section") - 1 - lax.axis_index("section")
    micro = step - SKEW * above
    active = jnp.logical_and(micro >= 0, micro < micros)
    return active, jnp.clip(micro, 0, micros - 1), above


def receive(micro, above, cot_ref, inc_ref, xups, raw):
    rows, width = raw.shape
    hidden = width // 2
    if inc_ref is None:
        raw[...] = cot_ref[micro]
        return
    message = inc_ref[...]
    raw[:, :hidden] = jnp.where(above == 0, cot_ref[micro, :, :hidden], message[:, :hidden])
    high = cot_ref[micro, :, hidden:]
    for far in reversed(range(len(xups))):
        coef = jnp.zeros((rows, 1), jnp.float32)
        for part in reversed(range(PARTS)):
            at = hidden + far * PARTS + part
            coef = coef + message[:, at : at + 1].astype(jnp.float32)
        value = (high.astype(jnp.float32) - xups[far][micro].astype(jnp.float32) * coef).astype(jnp.bfloat16)
        high = jnp.where(above > far, value, high)
    raw[:, hidden:] = high


def cut(length, raw, live, tiles):
    rows, width = raw.shape
    keep = lax.broadcasted_iota(jnp.int32, (rows, HEAD), 0) < length
    for tile in range(width // HEAD):
        cols = slice(tile * HEAD, (tile + 1) * HEAD)
        value = jnp.where(keep, raw[:, cols].astype(jnp.float32), 0.0).astype(jnp.bfloat16)
        if live is not None:
            live[:, cols] = value
        if tiles is not None:
            tiles[tile] = value


def layer(micro, above, weight_ref, x_ref, shared_ref, probs_ref, turned_ref, inv_ref, gain_ref, gacc_ref, inc_ref,
          raw, live, message_ref, gout_ref, grad_ref, grad_attn, scaled_ref):
    scale = SCORE_FACTOR / math.sqrt(HEAD)
    rows, width = raw.shape
    hidden = width // 2
    for start in range(0, hidden, CHUNK):
        turned = dot_nt(weight_ref[start : start + CHUNK, :], live[...])
        grad_attn[:, start : start + CHUNK] = turned.T.astype(jnp.bfloat16)
    inv = inv_ref[micro]
    inner = jnp.zeros((rows, HEAD), jnp.float32)
    for head in range(hidden // HEAD):
        cols = slice(head * HEAD, (head + 1) * HEAD)
        shared = shared_ref[micro, :, cols]
        probs = probs_ref[micro, head]
        grad_head = grad_attn[:, cols]
        grad_probs = dot_nt(grad_head, shared)
        delta = jnp.sum(probs * grad_probs, axis=1, keepdims=True)
        dscore = scale * probs * (grad_probs - delta)
        left = jnp.concatenate([(dscore + dscore.T).astype(jnp.bfloat16), turned_ref[micro, head]], axis=1)
        grad_shared = dot_nn(left, jnp.concatenate([shared, grad_head], axis=0))
        x_head = x_ref[micro, :, cols].astype(jnp.float32)
        gout_ref[:, cols] = gacc_ref[:, cols] + jnp.sum(grad_shared * (x_head * inv), axis=0, keepdims=True)
        scaled = grad_shared * gain_ref[:, cols]
        inner = inner + scaled * x_head
        scaled_ref[:, cols] = scaled
    inv = inv[:, :1]
    coef = inv * inv * inv * (jnp.sum(inner, axis=1, keepdims=True) / width)
    low = raw[:, :hidden].astype(jnp.float32) + inv * scaled_ref[...] - x_ref[micro, :, :hidden].astype(jnp.float32) * coef
    low = low.astype(jnp.bfloat16)
    grad_ref[:, :hidden] = low
    high = raw[:, hidden:].astype(jnp.float32) - x_ref[micro, :, hidden:].astype(jnp.float32) * coef
    grad_ref[:, hidden:] = high.astype(jnp.bfloat16)
    if message_ref is None:
        return
    message_ref[:, :hidden] = low
    lane = lax.broadcasted_iota(jnp.int32, (rows, HEAD), 1)
    if inc_ref is None:
        tail = jnp.zeros((rows, HEAD), jnp.float32)
    else:
        came = jnp.where(above == 0, 0.0, inc_ref[:, hidden:].astype(jnp.float32))
        tail = jnp.where(lane < PARTS, 0.0, pltpu.roll(came, PARTS, axis=1))
    rest = coef
    for part in range(PARTS):
        piece = rest.astype(jnp.bfloat16).astype(jnp.float32)
        tail = jnp.where(lane == part, piece, tail)
        rest = rest - piece
    message_ref[:, hidden:] = tail.astype(jnp.bfloat16)


def layer_step(step, table, fixed, gain_acc, incoming, xups, store, before, masked, raw=None):
    weight, inputs, upstream, shared, probs, turned, inv, gain_row = fixed
    micros, rows, width = inputs.shape
    hidden = width // 2
    half = micros // 2
    last = raw is not None
    named = {
        "weight": weight, "x": inputs, "cot": upstream, "shared": shared, "probs": probs, "turned": turned,
        "inv": inv, "gain": gain_row, "gacc": gain_acc, "store_in": store,
    }
    if last:
        named["raw"] = raw
    else:
        for far, xup in enumerate(xups):
            named[f"xup{far}"] = xup
        for index, part in masked.items():
            named[f"masked_in{index}"] = part
    if incoming is not None and not last:
        named["inc"] = incoming
    if before is not None:
        named["before"] = before
    row_shape = jax.ShapeDtypeStruct((rows, width), jnp.bfloat16)
    outs = {"grad": row_shape, "gout": jax.ShapeDtypeStruct((1, hidden), jnp.float32)}
    outs["store"] = jax.ShapeDtypeStruct(store.shape, store.dtype)
    if not last:
        outs["message"] = jax.ShapeDtypeStruct((rows, hidden + HEAD), jnp.bfloat16)
        for index, part in masked.items():
            outs[f"masked{index}"] = jax.ShapeDtypeStruct(part.shape, part.dtype)
    scratch = {
        "live": pltpu.VMEM((rows, width), jnp.bfloat16),
        "grad_attn": pltpu.VMEM((rows, hidden), jnp.bfloat16),
        "scaled": pltpu.VMEM((rows, hidden), jnp.float32),
        "sems": pltpu.SemaphoreType.DMA((2,)),
    }
    if not last:
        scratch["raw"] = pltpu.VMEM((rows, width), jnp.bfloat16)
        scratch["tiles"] = pltpu.VMEM((width // HEAD, rows, HEAD), jnp.bfloat16)
    keys = list(named) + list(outs) + list(scratch)

    def body(lengths, *refs):
        r = dict(zip(keys, refs))
        active, micro, above = place(step, micros)
        was_active, was_micro, _ = place(step - 1, micros)
        sems = r["sems"]
        if before is not None:
            flush = pltpu.make_async_copy(r["before"], r["store"].at[was_micro], sems.at[0])

            @pl.when(was_active)
            def _():
                flush.start()

        @pl.when(jnp.logical_not(active))
        def _():
            r["gout"][...] = r["gacc"][...]

        @pl.when(active)
        def _():
            length = lengths[0, micro]
            inc = r.get("inc")
            if last:
                cut(length, r["raw"], r["live"], None)
            else:
                receive(micro, above, r["cot"], inc, [r[f"xup{far}"] for far in range(len(xups))], r["raw"])
                cut(length, r["raw"], r["live"], r["tiles"])
                for index in masked:
                    @pl.when(micro // half == index)
                    def _():
                        pltpu.make_async_copy(
                            r["tiles"], r[f"masked{index}"].at[:, micro % half], sems.at[1]
                        ).start()
            layer(micro, above, r["weight"], r["x"], r["shared"], r["probs"], r["turned"], r["inv"], r["gain"],
                  r["gacc"], inc, r["raw"], r["live"], r.get("message"), r["gout"], r["grad"], r["grad_attn"],
                  r["scaled"])
            for index in masked:
                @pl.when(micro // half == index)
                def _():
                    pltpu.make_async_copy(
                        r["tiles"], r[f"masked{index}"].at[:, micro % half], sems.at[1]
                    ).wait()

        if before is not None:
            @pl.when(was_active)
            def _():
                flush.wait()

    places = list(named)
    results = list(outs)
    aliases = {1 + places.index("store_in"): results.index("store")}
    if not last:
        for index in masked:
            aliases[1 + places.index(f"masked_in{index}")] = results.index(f"masked{index}")
    spec = lambda key: FAR if key.startswith(("store", "masked")) else VMEM
    values = pl.pallas_call(
        body,
        name="layer_last" if last else "layer_step",
        in_specs=[SMEM] + [spec(key) for key in named],
        out_specs=[spec(key) for key in outs],
        out_shape=list(outs.values()),
        scratch_shapes=list(scratch.values()),
        input_output_aliases=aliases,
        compiler_params=pltpu.CompilerParams(vmem_limit_bytes=LIMIT),
        cost_estimate=pl.CostEstimate(flops=5_000_000_000, bytes_accessed=2_000_000, transcendentals=0),
    )(table, *named.values())
    return dict(zip(outs, values))


def receive_step(step, table, upstream, xups, incoming, masked):
    micros, rows, width = upstream.shape
    half = micros // 2
    far = len(xups)

    def body(lengths, inc_ref, cot_ref, *refs):
        xup_refs = refs[:far]
        masked_in, raw, masked_ref, tiles, sem = refs[far:]
        active, micro, above = place(step, micros)

        @pl.when(active)
        def _():
            receive(micro, above, cot_ref, inc_ref, xup_refs, raw)
            cut(lengths[0, micro], raw, None, tiles)
            copy = pltpu.make_async_copy(tiles, masked_ref.at[:, micro % half], sem)
            copy.start()
            copy.wait()

    return pl.pallas_call(
        body,
        name="receive_step",
        in_specs=[SMEM] + [VMEM] * (far + 2) + [FAR],
        out_specs=[VMEM, FAR],
        out_shape=[
            jax.ShapeDtypeStruct((rows, width), jnp.bfloat16),
            jax.ShapeDtypeStruct(masked.shape, masked.dtype),
        ],
        scratch_shapes=[pltpu.VMEM((width // HEAD, rows, HEAD), jnp.bfloat16), pltpu.SemaphoreType.DMA],
        input_output_aliases={3 + far: 1},
        compiler_params=pltpu.CompilerParams(vmem_limit_bytes=LIMIT),
        cost_estimate=pl.CostEstimate(flops=1_000_000, bytes_accessed=2_000_000, transcendentals=0),
    )(table, incoming, upstream, *xups, masked)


def flush_step(step, store, before):
    micros = store.shape[0]

    def body(before_ref, store_in, store_ref, sem):
        active, micro, _ = place(step, micros)

        @pl.when(active)
        def _():
            copy = pltpu.make_async_copy(before_ref, store_ref.at[micro], sem)
            copy.start()
            copy.wait()

    return pl.pallas_call(
        body,
        name="flush_step",
        in_specs=[VMEM, FAR],
        out_specs=FAR,
        out_shape=jax.ShapeDtypeStruct(store.shape, store.dtype),
        scratch_shapes=[pltpu.SemaphoreType.DMA],
        input_output_aliases={1: 0},
        compiler_params=pltpu.CompilerParams(vmem_limit_bytes=LIMIT),
    )(before, store)


def buffers(shapes):
    def body(*refs):
        pass

    return pl.pallas_call(
        body,
        name="buffers",
        out_specs=[FAR] * len(shapes),
        out_shape=[jax.ShapeDtypeStruct(shape, jnp.bfloat16) for shape in shapes],
    )()


def product(attended, columns, so_far=None, gain=None, owners=None):
    depth, hidden = attended.shape
    final = so_far is not None

    def body(*refs):
        if final:
            att_ref, col_ref, so_far_ref, gain_ref, out_ref, acc = refs
        else:
            att_ref, col_ref, acc = refs

        @pl.when(pl.program_id(0) == 0)
        def _():
            acc[...] = so_far_ref[...] if final else jnp.zeros_like(acc)

        acc[...] += dot_tn(col_ref[...], att_ref[...])

        if final:
            @pl.when(pl.program_id(0) == pl.num_programs(0) - 1)
            def _():
                own = hidden // owners
                for pair in range(owners // 2):
                    cols = slice(pair * 2 * own, (pair + 1) * 2 * own)
                    turned = acc[:, cols].T.astype(jnp.bfloat16)
                    gains = jnp.broadcast_to(gain_ref[:, cols], (PAD - own, HEAD)).astype(jnp.bfloat16)
                    for side in range(2):
                        out_ref[2 * pair + side, :own] = turned[side * own : (side + 1) * own]
                        out_ref[2 * pair + side, own:] = gains

    whole = pl.BlockSpec((HEAD, hidden), lambda i: (0, 0))
    in_specs = [pl.BlockSpec((DEPTH, hidden), lambda i: (i, 0)), pl.BlockSpec((DEPTH, HEAD), lambda i: (i, 0))]
    params = pltpu.CompilerParams(vmem_limit_bytes=16 << 20)
    cost = pl.CostEstimate(flops=2 * depth * hidden * HEAD, bytes_accessed=2 * depth * hidden, transcendentals=0)
    if not final:
        return pl.pallas_call(
            body, name="product", grid=(depth // DEPTH,), in_specs=in_specs, out_specs=whole,
            out_shape=jax.ShapeDtypeStruct((HEAD, hidden), jnp.float32), compiler_params=params, cost_estimate=cost,
        )(attended, columns)
    return pl.pallas_call(
        body,
        name="product_final",
        grid=(depth // DEPTH,),
        in_specs=in_specs + [whole, pl.BlockSpec((1, hidden), lambda i: (0, 0))],
        out_specs=pl.BlockSpec((owners, PAD, HEAD), lambda i: (0, 0, 0)),
        out_shape=jax.ShapeDtypeStruct((owners, PAD, HEAD), jnp.bfloat16),
        scratch_shapes=[pltpu.VMEM((HEAD, hidden), jnp.float32)],
        compiler_params=params,
        cost_estimate=cost,
    )(attended, columns, so_far, gain)


def unpack(block, own):
    sources = block.shape[0]

    def body(block_ref, proj_ref, gain_ref):
        total = jnp.zeros((1, HEAD), jnp.float32)
        for source in range(sources):
            proj_ref[:, source * HEAD : (source + 1) * HEAD] = block_ref[source, :own].astype(jnp.float32)
            total = total + block_ref[source, own : own + 16].astype(jnp.float32)[:1]
        odd = lax.rem(lax.axis_index(DP), 2) == 1
        gain_ref[...] = jnp.where(odd, total[:, own:], total[:, :own])

    return pl.pallas_call(
        body,
        name="unpack",
        in_specs=[VMEM],
        out_specs=[VMEM] * 2,
        out_shape=[
            jax.ShapeDtypeStruct((own, sources * HEAD), jnp.float32),
            jax.ShapeDtypeStruct((1, own), jnp.float32),
        ],
        compiler_params=pltpu.CompilerParams(vmem_limit_bytes=LIMIT),
    )(block)


def per_device(saved_inputs, cotangent, out_proj, norm_gain, lengths):
    sections = lax.axis_size("section")
    replicas = lax.axis_size(DP)
    gain_row = norm_gain
    inputs = saved_inputs[0, 0]
    micros, rows, width = inputs.shape
    hidden = out_proj.shape[1]
    tiles = width // HEAD
    half = micros // 2

    own_up = inputs[:, :, hidden:]
    near = lax.ppermute(own_up, "section", [(3, 2), (2, 1), (1, 0)])
    round_once = lax.ppermute(own_up, "section", [(3, 0), (2, 3)])
    round_twice = lax.ppermute(round_once, "section", [(0, 1), (3, 0)])
    xups = [near, round_twice, round_once]

    weight, inputs, upstream, shared, probs, turned, inv, *attended = prelude(
        lengths, inputs, gain_row, out_proj[0], cotangent[0]
    )
    gathered = [lax.all_gather(part, DP, axis=0, tiled=True) for part in attended]
    fixed = (weight, inputs, upstream, shared, probs, turned, inv, gain_row)

    store, *masked = buffers([(micros, rows, width)] + [(tiles, half, rows, HEAD)] * 2)
    gain_acc = jnp.zeros((1, hidden), jnp.float32)

    steps = SKEW * (sections - 1) + micros
    arriving = {}
    before = None

    def exchange(part):
        got = lax.all_to_all(part.reshape(tiles, half * rows, HEAD), DP, 0, 0, tiled=True)
        return got.reshape(replicas * half * rows, HEAD)

    for step in range(steps):
        incoming = arriving.get(step)
        depth = min(step // SKEW, sections - 1)
        if step == steps - 1:
            raw, masked[1] = receive_step(step, lengths, upstream, xups, incoming, masked[1])
            raw, columns = lax.optimization_barrier((raw, columns))
            late_columns = exchange(masked[1])
            done = layer_step(step, lengths, fixed, gain_acc, incoming, [], store, before, {}, raw)
            gain_acc = done["gout"]
            store = flush_step(step, done["store"], done["grad"])
            break
        used = {index: masked[index] for index in ((0, 1) if step < steps - half else (1,))}
        done = layer_step(step, lengths, fixed, gain_acc, incoming, xups[:depth], store, before, used)
        gain_acc, store, before = done["gout"], done["store"], done["grad"]
        for index in used:
            masked[index] = done[f"masked{index}"]
        route = [
            (src, src - 1)
            for src in range(1, sections)
            if 0 <= step - SKEW * (sections - 1 - src) < micros
        ]
        if route:
            arriving[step + SKEW] = lax.ppermute(done["message"], "section", route)
        if step == steps - half - 1:
            columns = exchange(masked[0])

    so_far = product(gathered[0], columns)
    packed = product(gathered[1], late_columns, so_far, gain_acc, replicas)
    block = lax.all_to_all(packed, DP, 0, 0, tiled=True)
    proj, gain = unpack(block, hidden // replicas)
    return (store[None, None], proj[None], gain)


def solution(mesh):
    placed = (
        P("section", "dp", None, None, None),
        P("dp", None, None, None),
        P("section", None, None),
        P("section", None),
        P("dp", None),
    )
    return jax.shard_map(
        per_device,
        mesh=mesh,
        in_specs=placed,
        out_specs=(
            P("section", "dp", None, None, None),
            P("section", "dp", None),
            P("section", "dp"),
        ),
        check_vma=False,
    )
```

```python
import math

import jax
import jax.numpy as jnp
from jax import lax
from jax.experimental import pallas as pl
from jax.experimental.pallas import tpu as pltpu
from jax.sharding import PartitionSpec as P

HEAD = 128
NORM_EPS = 1e-06
SCORE_FACTOR = 0.6
MASKED_SCORE = -1e30
DP = "dp"
SKEW = 2
CHUNK = 256
LIMIT = 56 << 20
PARTS = 3
DEPTH = 512
PAD = 80

VMEM = pl.BlockSpec(memory_space=pltpu.VMEM)
SMEM = pl.BlockSpec(memory_space=pltpu.SMEM)
FAR = pl.BlockSpec(memory_space=pl.ANY)


def dot_nt(a, b):
    return lax.dot_general(a, b, (((1,), (1,)), ((), ())), preferred_element_type=jnp.float32)


def dot_nn(a, b):
    return lax.dot_general(a, b, (((1,), (0,)), ((), ())), preferred_element_type=jnp.float32)


def dot_tn(a, b):
    return lax.dot_general(a, b, (((0,), (0,)), ((), ())), preferred_element_type=jnp.float32)


def kernel(name, body, operands, outs, scratch, sems, aliases=(), near=(), flops=0, moved=0):
    keys = ["lengths", *list(operands)[1:], *outs, *scratch, "sems"]

    def run(*refs):
        body(dict(zip(keys, refs)))

    names = list(operands)
    spec = lambda key: VMEM if key in near else FAR
    values = pl.pallas_call(
        run,
        name=name,
        in_specs=[SMEM] + [spec(key) for key in names[1:]],
        out_specs=[spec(key) for key in outs],
        out_shape=[jax.ShapeDtypeStruct(*item) for item in outs.values()],
        scratch_shapes=[pltpu.VMEM(*item) for item in scratch.values()] + [pltpu.SemaphoreType.DMA((sems,))],
        input_output_aliases={names.index(a): list(outs).index(b) for a, b in aliases},
        compiler_params=pltpu.CompilerParams(vmem_limit_bytes=LIMIT),
        cost_estimate=pl.CostEstimate(flops=flops, bytes_accessed=moved, transcendentals=0),
    )(*operands.values())
    return dict(zip(outs, values))


def prelude(lengths, inputs, gain_row):
    micros, rows, width = inputs.shape
    hidden = gain_row.shape[1]
    heads = hidden // HEAD
    scale = SCORE_FACTOR / math.sqrt(HEAD)

    def body(r):
        sems = r["sems"]
        loads = [
            pltpu.make_async_copy(r["inputs"].at[micro], r["x"].at[micro], sems.at[micro]) for micro in range(micros)
        ]
        for load in loads:
            load.start()
        writes = [pltpu.make_async_copy(r["x"].at[:, :, pl.ds(hidden, width - hidden)], r["upper"], sems.at[micros])]
        for micro in range(micros):
            loads[micro].wait()
        writes[0].start()
        for micro in range(micros):
            x = r["x"][micro].astype(jnp.float32)
            inv = lax.rsqrt(jnp.mean(x * x, axis=1, keepdims=True) + NORM_EPS)
            r["inv_v"][micro] = jnp.broadcast_to(inv, (rows, HEAD))
            r["shared_v"][micro] = (x[:, :hidden] * inv * r["gain"][...]).astype(jnp.bfloat16)
            live = lax.broadcasted_iota(jnp.int32, (rows, rows), 1) < r["lengths"][0, micro]
            for head in range(heads):
                cols = slice(head * HEAD, (head + 1) * HEAD)
                shared = r["shared_v"][micro, :, cols]
                scores = jnp.where(live, dot_nt(shared, shared) * scale, MASKED_SCORE)
                exponent = jnp.exp(scores - jnp.max(scores, axis=1, keepdims=True))
                probs = exponent / jnp.sum(exponent, axis=1, keepdims=True)
                r["probs_v"][micro, head] = probs
                r["turned_v"][micro, head] = probs.T.astype(jnp.bfloat16)
                r["attended_v"][micro, :, cols] = dot_nn(probs.astype(jnp.bfloat16), shared).astype(jnp.bfloat16)
            base = micros + 1 + 5 * micro
            for index, key in enumerate(("attended", "shared", "probs", "turned", "inv")):
                write = pltpu.make_async_copy(r[key + "_v"].at[micro], r[key].at[micro], sems.at[base + index])
                write.start()
                writes.append(write)
        for write in writes:
            write.wait()

    outs = {
        "attended": ((micros, rows, hidden), jnp.bfloat16),
        "shared": ((micros, rows, hidden), jnp.bfloat16),
        "probs": ((micros, heads, rows, rows), jnp.float32),
        "turned": ((micros, heads, rows, rows), jnp.bfloat16),
        "inv": ((micros, rows, HEAD), jnp.float32),
        "upper": ((micros, rows, width - hidden), jnp.bfloat16),
    }
    scratch = {"x": (inputs.shape, jnp.bfloat16)}
    for key in ("attended", "shared", "probs", "turned", "inv"):
        scratch[key + "_v"] = outs[key]
    return kernel(
        "prelude", body, {"lengths": lengths, "inputs": inputs, "gain": gain_row}, outs, scratch,
        6 * micros + 1, near=("gain",), flops=500_000_000, moved=8_000_000,
    )


def place(step, micros):
    above = lax.axis_size("section") - 1 - lax.axis_index("section")
    micro = step - SKEW * above
    active = jnp.logical_and(micro >= 0, micro < micros)
    return active, jnp.clip(micro, 0, micros - 1), above


def upper_product(lengths, weight, rows_from, least):
    hidden, width = weight.shape
    micros, rows, wide = rows_from.shape
    upper = width - hidden
    chunks = hidden // CHUNK

    def body(r):
        sems = r["sems"]
        above = lax.axis_size("section") - 1 - lax.axis_index("section")

        @pl.when(above >= least)
        def _():
            given = pltpu.make_async_copy(r["given"].at[:, :, pl.ds(wide - upper, upper)], r["rows"], sems.at[chunks])
            given.start()
            loads = [
                pltpu.make_async_copy(
                    r["weight"].at[pl.ds(index * CHUNK, CHUNK), pl.ds(hidden, upper)], r["block"].at[index], sems.at[index]
                )
                for index in range(chunks)
            ]
            for load in loads:
                load.start()
            given.wait()
            for index in range(chunks):
                loads[index].wait()
                turned = dot_nt(r["block"][index], r["rows"][...].reshape(micros * rows, upper))
                r["total"][:, :, index * CHUNK : (index + 1) * CHUNK] = turned.T.reshape(micros, rows, CHUNK)
            write = pltpu.make_async_copy(r["total"], r["out"], sems.at[chunks + 1])
            write.start()
            write.wait()

    shape = ((micros, rows, hidden), jnp.float32)
    return kernel(
        "upper_product", body, {"lengths": lengths, "weight": weight, "given": rows_from}, {"out": shape},
        {
            "rows": ((micros, rows, upper), jnp.bfloat16),
            "block": ((chunks, CHUNK, upper), jnp.bfloat16),
            "total": shape,
        },
        chunks + 2, flops=1_600_000_000, moved=10_000_000,
    )["out"]


def coefficients(message, hidden, count):
    found = []
    for far in range(count):
        coef = jnp.zeros((message.shape[0], 1), jnp.float32)
        for part in reversed(range(PARTS)):
            at = hidden + far * PARTS + part
            coef = coef + message[:, at : at + 1].astype(jnp.float32)
        found.append(coef)
    return found


def rebuild(above, raw, r, coefs, hidden):
    high = raw[:, hidden:]
    for far in reversed(range(len(coefs))):
        value = (high.astype(jnp.float32) - r[f"xup{far}_v"][...].astype(jnp.float32) * coefs[far]).astype(jnp.bfloat16)
        high = jnp.where(above > far, value, high)
    raw[:, hidden:] = high


def cut(length, raw, tiles):
    rows, width = raw.shape
    keep = lax.broadcasted_iota(jnp.int32, (rows, HEAD), 0) < length
    for tile in range(width // HEAD):
        value = raw[:, tile * HEAD : (tile + 1) * HEAD].astype(jnp.float32)
        tiles[tile] = jnp.where(keep, value, 0.0).astype(jnp.bfloat16)


def layer_step(step, lengths, state, incoming, xups, uppers, gain_acc, store, masked, last):
    micros, rows, width = state["inputs"].shape
    hidden = state["weight"].shape[0]
    heads = hidden // HEAD
    chunks = hidden // CHUNK
    count = len(xups)
    scale = SCORE_FACTOR / math.sqrt(HEAD)

    operands = {"lengths": lengths, **state, "gacc": gain_acc, "store_in": store}
    if masked is not None:
        operands["masked_in"] = masked
    if incoming is not None:
        operands["inc"] = incoming
    for far in range(count):
        operands[f"xup{far}"] = xups[far]
        operands[f"upper{far}"] = uppers[far]
    outs = {"gout": ((1, hidden), jnp.float32), "store": (store.shape, store.dtype)}
    aliases = [("store_in", "store")]
    if masked is not None:
        outs["masked"] = (masked.shape, masked.dtype)
        aliases.append(("masked_in", "masked"))
    if not last:
        outs["message"] = ((rows, hidden + HEAD), jnp.bfloat16)
    scratch = {
        "raw": ((rows, width), jnp.bfloat16),
        "block": ((chunks, CHUNK, hidden), jnp.bfloat16),
        "base_v": ((rows, hidden), jnp.float32),
        "shared_v": ((rows, hidden), jnp.bfloat16),
        "probs_v": ((heads, rows, rows), jnp.float32),
        "turned_v": ((heads, rows, rows), jnp.bfloat16),
        "inv_v": ((rows, HEAD), jnp.float32),
        "x_v": ((rows, width), jnp.bfloat16),
        "grad_attn": ((rows, hidden), jnp.bfloat16),
        "scaled": ((rows, hidden), jnp.float32),
        "grad": ((rows, width), jnp.bfloat16),
    }
    if masked is not None:
        scratch["tiles"] = ((width // HEAD, rows, HEAD), jnp.bfloat16)
    for far in range(count):
        scratch[f"xup{far}_v"] = ((rows, width - hidden), jnp.bfloat16)
        scratch[f"upper{far}_v"] = ((rows, hidden), jnp.float32)

    def body(r):
        active, micro, above = place(step, micros)
        sems = r["sems"]
        used = []

        def copy(source, target):
            made = pltpu.make_async_copy(source, target, sems.at[len(used)])
            used.append(made)
            return made

        def guarded(far, action):
            @pl.when(above > far)
            def _():
                action()

        @pl.when(jnp.logical_not(active))
        def _():
            r["gout"][...] = r["gacc"][...]

        @pl.when(active)
        def _():
            cot = copy(r["cot"].at[micro], r["raw"])
            cot.start()
            base = copy(r["base"].at[micro], r["base_v"])
            base.start()
            extra = [copy(r[f"upper{far}"].at[micro], r[f"upper{far}_v"]) for far in range(count)]
            for far in range(count):
                guarded(far, extra[far].start)
            blocks = [
                copy(r["weight"].at[pl.ds(index * CHUNK, CHUNK), pl.ds(0, hidden)], r["block"].at[index])
                for index in range(chunks)
            ]
            for block in blocks[:3]:
                block.start()
            rest = {}
            for key in ("probs", "shared", "turned", "inv"):
                rest[key] = copy(r[key].at[micro], r[key + "_v"])
            rest["x"] = copy(r["inputs"].at[micro], r["x_v"])
            ups = [copy(r[f"xup{far}"].at[micro], r[f"xup{far}_v"]) for far in range(count)]
            for block in blocks[3:]:
                block.start()
            for made in rest.values():
                made.start()
            for far in range(count):
                guarded(far, ups[far].start)

            cot.wait()
            if incoming is not None:
                @pl.when(above > 0)
                def _():
                    r["raw"][:, :hidden] = r["inc"][:, :hidden]

                coefs = coefficients(r["inc"][...], hidden, count)
            else:
                coefs = []
            base.wait()
            for far in range(count):
                @pl.when(above > far)
                def _():
                    extra[far].wait()
                    r["base_v"][...] = r["base_v"][...] - coefs[far] * r[f"upper{far}_v"][...]

            length = r["lengths"][0, micro]
            keep = lax.broadcasted_iota(jnp.int32, (rows, CHUNK), 0) < length
            for index in range(chunks):
                cols = slice(index * CHUNK, (index + 1) * CHUNK)
                blocks[index].wait()
                turned = dot_nt(r["block"][index], r["raw"][:, :hidden])
                value = jnp.where(keep, turned.T + r["base_v"][:, cols], 0.0)
                r["grad_attn"][:, cols] = value.astype(jnp.bfloat16)
            for made in rest.values():
                made.wait()
            inv = r["inv_v"][...]
            inner = jnp.zeros((rows, HEAD), jnp.float32)
            for head in range(heads):
                cols = slice(head * HEAD, (head + 1) * HEAD)
                shared = r["shared_v"][:, cols]
                probs = r["probs_v"][head]
                grad_head = r["grad_attn"][:, cols]
                grad_probs = dot_nt(grad_head, shared)
                delta = jnp.sum(probs * grad_probs, axis=1, keepdims=True)
                dscore = scale * probs * (grad_probs - delta)
                left = jnp.concatenate([(dscore + dscore.T).astype(jnp.bfloat16), r["turned_v"][head]], axis=1)
                grad_shared = dot_nn(left, jnp.concatenate([shared, grad_head], axis=0))
                x_head = r["x_v"][:, cols].astype(jnp.float32)
                gain_term = jnp.sum(grad_shared * (x_head * inv), axis=0, keepdims=True)
                r["gout"][:, cols] = r["gacc"][:, cols] + gain_term
                scaled = grad_shared * r["gain"][:, cols]
                inner = inner + scaled * x_head
                r["scaled"][:, cols] = scaled
            inv = inv[:, :1]
            coef = inv * inv * inv * (jnp.sum(inner, axis=1, keepdims=True) / width)
            low = r["raw"][:, :hidden].astype(jnp.float32) + inv * r["scaled"][...]
            low = (low - r["x_v"][:, :hidden].astype(jnp.float32) * coef).astype(jnp.bfloat16)
            r["grad"][:, :hidden] = low
            if not last:
                r["message"][:, :hidden] = low
                lane = lax.broadcasted_iota(jnp.int32, (rows, HEAD), 1)
                if incoming is None:
                    tail = jnp.zeros((rows, HEAD), jnp.float32)
                else:
                    came = jnp.where(above == 0, 0.0, r["inc"][:, hidden:].astype(jnp.float32))
                    tail = jnp.where(lane < PARTS, 0.0, pltpu.roll(came, PARTS, axis=1))
                left_over = coef
                for part in range(PARTS):
                    piece = left_over.astype(jnp.bfloat16).astype(jnp.float32)
                    tail = jnp.where(lane == part, piece, tail)
                    left_over = left_over - piece
                r["message"][:, hidden:] = tail.astype(jnp.bfloat16)
            for far in range(count):
                guarded(far, ups[far].wait)
            rebuild(above, r["raw"], r, coefs, hidden)
            high = r["raw"][:, hidden:].astype(jnp.float32) - r["x_v"][:, hidden:].astype(jnp.float32) * coef
            r["grad"][:, hidden:] = high.astype(jnp.bfloat16)
            keepers = [copy(r["grad"], r["store"].at[micro])]
            keepers[0].start()
            if masked is not None:
                cut(length, r["raw"], r["tiles"])
                keepers.append(copy(r["tiles"], r["masked"].at[:, micro]))
                keepers[1].start()
            for made in keepers:
                made.wait()

    return kernel(
        "layer_step", body, operands, outs, scratch, chunks + 2 * count + 12, aliases,
        near=("gain", "gacc", "gout", "inc", "message"), flops=3_000_000_000, moved=14_000_000,
    )


def receive_step(step, lengths, cot, incoming, xups, masked):
    micros, rows, width = cot.shape
    hidden = incoming.shape[1] - HEAD
    count = len(xups)
    operands = {"lengths": lengths, "cot": cot, "inc": incoming, "masked_in": masked}
    scratch = {
        "raw": ((rows, width), jnp.bfloat16),
        "tiles": ((width // HEAD, rows, HEAD), jnp.bfloat16),
    }
    for far in range(count):
        operands[f"xup{far}"] = xups[far]
        scratch[f"xup{far}_v"] = ((rows, width - hidden), jnp.bfloat16)

    def body(r):
        active, micro, above = place(step, micros)
        sems = r["sems"]

        @pl.when(active)
        def _():
            loads = [
                pltpu.make_async_copy(r["cot"].at[micro], r["raw"], sems.at[1]),
            ]
            for far in range(count):
                loads.append(pltpu.make_async_copy(r[f"xup{far}"].at[micro], r[f"xup{far}_v"], sems.at[3 + far]))
            for load in loads:
                load.start()
            for load in loads:
                load.wait()

            @pl.when(above > 0)
            def _():
                r["raw"][:, :hidden] = r["inc"][:, :hidden]

            rebuild(above, r["raw"], r, coefficients(r["inc"][...], hidden, count), hidden)
            cut(r["lengths"][0, micro], r["raw"], r["tiles"])
            write = pltpu.make_async_copy(r["tiles"], r["masked"].at[:, micro], sems.at[2])
            write.start()
            write.wait()

    return kernel(
        "receive_step", body, operands, {"masked": (masked.shape, masked.dtype)}, scratch, 3 + count,
        [("masked_in", "masked")], near=("inc",), flops=1_000_000, moved=2_000_000,
    )["masked"]


def buffers(lengths, shapes):
    return kernel(
        "buffers", lambda r: None, {"lengths": lengths}, {key: (shape, jnp.bfloat16) for key, shape in shapes.items()},
        {}, 1,
    )


def product(attended, columns, gain, owners):
    depth, hidden = attended.shape
    own = hidden // owners

    def body(att_ref, col_ref, gain_ref, out_ref, acc):
        @pl.when(pl.program_id(0) == 0)
        def _():
            acc[...] = jnp.zeros_like(acc)

        acc[...] += dot_tn(col_ref[...], att_ref[...])

        @pl.when(pl.program_id(0) == pl.num_programs(0) - 1)
        def _():
            for pair in range(owners // 2):
                cols = slice(pair * 2 * own, (pair + 1) * 2 * own)
                turned = acc[:, cols].T.astype(jnp.bfloat16)
                gains = jnp.broadcast_to(gain_ref[:, cols], (PAD - own, HEAD)).astype(jnp.bfloat16)
                for side in range(2):
                    out_ref[2 * pair + side, :own] = turned[side * own : (side + 1) * own]
                    out_ref[2 * pair + side, own:] = gains

    return pl.pallas_call(
        body,
        name="product",
        grid=(depth // DEPTH,),
        in_specs=[
            pl.BlockSpec((DEPTH, hidden), lambda i: (i, 0)),
            pl.BlockSpec((DEPTH, HEAD), lambda i: (i, 0)),
            pl.BlockSpec((1, hidden), lambda i: (0, 0)),
        ],
        out_specs=pl.BlockSpec((owners, PAD, HEAD), lambda i: (0, 0, 0)),
        out_shape=jax.ShapeDtypeStruct((owners, PAD, HEAD), jnp.bfloat16),
        scratch_shapes=[pltpu.VMEM((HEAD, hidden), jnp.float32)],
        compiler_params=pltpu.CompilerParams(vmem_limit_bytes=LIMIT),
        cost_estimate=pl.CostEstimate(
            flops=2 * depth * hidden * HEAD, bytes_accessed=2 * depth * hidden, transcendentals=0
        ),
    )(attended, columns, gain)


def unpack(block, own):
    sources = block.shape[0]

    def body(block_ref, proj_ref, gain_ref):
        total = jnp.zeros((1, HEAD), jnp.float32)
        for source in range(sources):
            proj_ref[:, source * HEAD : (source + 1) * HEAD] = block_ref[source, :own].astype(jnp.float32)
            total = total + block_ref[source, own : own + 16].astype(jnp.float32)[:1]
        odd = lax.rem(lax.axis_index(DP), 2) == 1
        gain_ref[...] = jnp.where(odd, total[:, own:], total[:, :own])

    return pl.pallas_call(
        body,
        name="unpack",
        in_specs=[VMEM],
        out_specs=[VMEM] * 2,
        out_shape=[
            jax.ShapeDtypeStruct((own, sources * HEAD), jnp.float32),
            jax.ShapeDtypeStruct((1, own), jnp.float32),
        ],
        compiler_params=pltpu.CompilerParams(vmem_limit_bytes=LIMIT),
    )(block)


def per_device(saved_inputs, cotangent, out_proj, norm_gain, lengths):
    sections = lax.axis_size("section")
    replicas = lax.axis_size(DP)
    inputs = saved_inputs[0, 0]
    cot = cotangent[0]
    weight = out_proj[0]
    micros, rows, width = inputs.shape
    hidden = weight.shape[0]
    tiles = width // HEAD

    first = prelude(lengths, inputs, norm_gain)
    attended = first.pop("attended").reshape(micros * rows, hidden)
    own_up = first.pop("upper")
    round_once = lax.ppermute(own_up, "section", [(3, 0), (2, 3)])
    near = lax.ppermute(own_up, "section", [(3, 2), (2, 1), (1, 0)])
    round_twice = lax.ppermute(round_once, "section", [(0, 1), (3, 0)])
    xups = [near, round_twice, round_once]
    gathered = lax.all_gather(attended, DP, axis=0, tiled=True)

    base = upper_product(lengths, weight, cot, 0)
    state = {"weight": weight, "inputs": inputs, "cot": cot, "base": base, "gain": norm_gain, **first}
    kept = buffers(lengths, {"store": (micros, rows, width), "masked": (tiles, micros, rows, HEAD)})
    store, masked = kept["store"], kept["masked"]
    gain_acc = jnp.zeros((1, hidden), jnp.float32)

    steps = SKEW * (sections - 1) + micros
    arriving = {}
    uppers = []
    for step in range(steps):
        incoming = arriving.get(step)
        last = step == steps - 1
        depth = min(step // SKEW, sections - 1)
        while len(uppers) < depth:
            uppers.append(upper_product(lengths, weight, xups[len(uppers)], len(uppers) + 1))
        if last:
            masked = receive_step(step, lengths, cot, incoming, xups, masked)
            columns = lax.all_to_all(masked.reshape(tiles, micros * rows, HEAD), DP, 0, 0, tiled=True)
        done = layer_step(
            step, lengths, state, incoming, xups[:depth], uppers, gain_acc, store, None if last else masked, last
        )
        gain_acc, store = done["gout"], done["store"]
        if last:
            break
        masked = done["masked"]
        route = [
            (src, src - 1)
            for src in range(1, sections)
            if 0 <= step - SKEW * (sections - 1 - src) < micros
        ]
        if route:
            arriving[step + SKEW] = lax.ppermute(done["message"], "section", route)

    packed = product(gathered, columns.reshape(replicas * micros * rows, HEAD), gain_acc, replicas)
    block = lax.all_to_all(packed, DP, 0, 0, tiled=True)
    proj, gain = unpack(block, hidden // replicas)
    return (store[None, None], proj[None], gain)


def solution(mesh):
    placed = (
        P("section", "dp", None, None, None),
        P("dp", None, None, None),
        P("section", None, None),
        P("section", None),
        P("dp", None),
    )
    return jax.shard_map(
        per_device,
        mesh=mesh,
        in_specs=placed,
        out_specs=(
            P("section", "dp", None, None, None),
            P("section", "dp", None),
            P("section", "dp"),
        ),
        check_vma=False,
    )
```

```python
import math
from types import SimpleNamespace

import jax
import jax.numpy as jnp
from jax import lax
from jax.experimental import pallas as pl
from jax.experimental.pallas import tpu as pltpu
from jax.sharding import PartitionSpec as P

HEAD = 128
NORM_EPS = 1e-06
SCORE_FACTOR = 0.6
MASKED_SCORE = -1e30
DP = "dp"
SKEW = 2
CHUNK = 256
LIMIT = 56 << 20
TIGHT = 10 << 20
WINDOW = 2
PARTS = 3
DEPTH = 512
PAD = 80

VMEM = pl.BlockSpec(memory_space=pltpu.VMEM)
SMEM = pl.BlockSpec(memory_space=pltpu.SMEM)
FAR = pl.BlockSpec(memory_space=pl.ANY)


def dot_nt(a, b):
    return lax.dot_general(a, b, (((1,), (1,)), ((), ())), preferred_element_type=jnp.float32)


def dot_nn(a, b):
    return lax.dot_general(a, b, (((1,), (0,)), ((), ())), preferred_element_type=jnp.float32)


def dot_tn(a, b):
    return lax.dot_general(a, b, (((0,), (0,)), ((), ())), preferred_element_type=jnp.float32)


def kernel(name, body, operands, outs, scratch, sems, aliases=(), near=(), flops=0, moved=0, limit=LIMIT):
    sizes = {key: len(value) for key, value in (*operands.items(), *scratch.items()) if isinstance(value, list)}

    def flat(items):
        return [one for value in items.values() for one in (value if isinstance(value, list) else [value])]

    def run(*refs):
        refs = iter(refs)
        named = {}
        for key in (*operands, *outs, *scratch):
            named[key] = [next(refs) for _ in range(sizes[key])] if key in sizes else next(refs)
        body(SimpleNamespace(**named, sems=next(refs)))

    order = {key: sum(sizes.get(k, 1) for k in list(operands)[:i]) for i, key in enumerate(operands)}
    in_specs = []
    for key in operands:
        in_specs += [SMEM if key == "lengths" else VMEM if key in near else FAR] * sizes.get(key, 1)
    values = pl.pallas_call(
        run,
        name=name,
        in_specs=in_specs,
        out_specs=[VMEM if key in near else FAR for key in outs],
        out_shape=[jax.ShapeDtypeStruct(*item) for item in outs.values()],
        scratch_shapes=[pltpu.VMEM(*item) for item in flat(scratch)] + [pltpu.SemaphoreType.DMA((sems,))],
        input_output_aliases={order[key + "_in"]: list(outs).index(key) for key in aliases},
        compiler_params=pltpu.CompilerParams(vmem_limit_bytes=limit),
        cost_estimate=pl.CostEstimate(flops=flops, bytes_accessed=moved, transcendentals=0),
    )(*flat(operands))
    return dict(zip(outs, values))


def prelude(lengths, inputs, gain):
    micros, rows, width = inputs.shape
    hidden = gain.shape[1]
    heads = hidden // HEAD
    scale = SCORE_FACTOR / math.sqrt(HEAD)

    def body(r):
        loads = [
            pltpu.make_async_copy(r.inputs.at[micro], r.x.at[micro], r.sems.at[micro]) for micro in range(micros)
        ]
        for load in loads:
            load.start()
        writes = [pltpu.make_async_copy(r.x.at[:, :, pl.ds(hidden, width - hidden)], r.upper, r.sems.at[micros])]
        for load in loads:
            load.wait()
        writes[0].start()
        for micro in range(micros):
            x = r.x[micro].astype(jnp.float32)
            inv = lax.rsqrt(jnp.mean(x * x, axis=1, keepdims=True) + NORM_EPS)
            r.inv_v[micro] = jnp.broadcast_to(inv, (rows, HEAD))
            r.shared_v[micro] = (x[:, :hidden] * inv * r.gain[...]).astype(jnp.bfloat16)
            live = lax.broadcasted_iota(jnp.int32, (rows, rows), 1) < r.lengths[0, micro]
            for head in range(heads):
                cols = slice(head * HEAD, (head + 1) * HEAD)
                shared = r.shared_v[micro, :, cols]
                scores = jnp.where(live, dot_nt(shared, shared) * scale, MASKED_SCORE)
                exponent = jnp.exp(scores - jnp.max(scores, axis=1, keepdims=True))
                probs = exponent / jnp.sum(exponent, axis=1, keepdims=True)
                r.probs_v[micro, head] = probs
                r.turned_v[micro, head] = probs.T.astype(jnp.bfloat16)
                r.attended_v[micro, :, cols] = dot_nn(probs.astype(jnp.bfloat16), shared).astype(jnp.bfloat16)
            pairs = [
                (r.attended_v, r.attended), (r.shared_v, r.shared), (r.probs_v, r.probs), (r.turned_v, r.turned),
                (r.inv_v, r.inv),
            ]
            for index, (source, target) in enumerate(pairs):
                sem = r.sems.at[micros + 1 + len(pairs) * micro + index]
                writes.append(pltpu.make_async_copy(source.at[micro], target.at[micro], sem))
                writes[-1].start()
        for write in writes:
            write.wait()

    wide = ((micros, rows, hidden), jnp.bfloat16)
    square = (micros, heads, rows, rows)
    outs = dict(
        attended=wide, shared=wide, probs=(square, jnp.float32), turned=(square, jnp.bfloat16),
        inv=((micros, rows, HEAD), jnp.float32), upper=((micros, rows, width - hidden), jnp.bfloat16),
    )
    scratch = dict(
        x=(inputs.shape, jnp.bfloat16), attended_v=wide, shared_v=wide, probs_v=outs["probs"],
        turned_v=outs["turned"], inv_v=outs["inv"],
    )
    return kernel(
        "prelude", body, dict(lengths=lengths, inputs=inputs, gain=gain), outs, scratch,
        6 * micros + 1, near=("gain",), flops=500_000_000, moved=8_000_000,
    )


def place(step, micros):
    above = lax.axis_size("section") - 1 - lax.axis_index("section")
    micro = step - SKEW * above
    active = jnp.logical_and(micro >= 0, micro < micros)
    return active, jnp.clip(micro, 0, micros - 1), above


def turned_dot(weight, rows_from, micros):
    turned = dot_nt(weight, rows_from).T
    return turned.reshape(micros, turned.shape[0] // micros, turned.shape[1])


def load_weight(lengths, weight, cot):
    hidden, width = weight.shape
    micros, rows, _ = cot.shape
    chunks = hidden // CHUNK

    def body(r):
        given = pltpu.make_async_copy(r.cot.at[:, :, pl.ds(hidden, width - hidden)], r.given, r.sems.at[chunks])
        given.start()
        loads = []
        for index in range(chunks):
            part = pl.ds(index * CHUNK, CHUNK)
            loads.append(pltpu.make_async_copy(r.weight.at[part], r.kept.at[part], r.sems.at[index]))
        for load in loads[:WINDOW]:
            load.start()
        given.wait()
        writes = []
        for index in range(chunks):
            loads[index].wait()
            if index + WINDOW < chunks:
                loads[index + WINDOW].start()
            part = slice(index * CHUNK, (index + 1) * CHUNK)
            r.total[:, :, part] = turned_dot(
                r.kept[part, hidden:], r.given[...].reshape(micros * rows, width - hidden), micros
            )
            if index % 2:
                span = pl.ds((index - 1) * CHUNK, 2 * CHUNK)
                sem = r.sems.at[chunks + 1 + index // 2]
                writes.append(pltpu.make_async_copy(r.total.at[:, :, span], r.base.at[:, :, span], sem))
                writes[-1].start()
        for write in writes:
            write.wait()

    shape = ((micros, rows, hidden), jnp.float32)
    return kernel(
        "load_weight", body, dict(lengths=lengths, weight=weight, cot=cot),
        dict(kept=(weight.shape, jnp.bfloat16), base=shape),
        dict(given=((micros, rows, width - hidden), jnp.bfloat16), total=shape),
        chunks + 1 + chunks // 2, near=("kept",), flops=1_600_000_000, moved=22_000_000, limit=34 << 20,
    )


def upper_product(lengths, kept, given, least):
    hidden, width = kept.shape
    micros, rows, upper = given.shape
    chunks = hidden // CHUNK

    def body(r):
        above = lax.axis_size("section") - 1 - lax.axis_index("section")

        @pl.when(above >= least)
        def _():
            load = pltpu.make_async_copy(r.given, r.given_v, r.sems.at[0])
            load.start()
            load.wait()
            writes = []
            for index in range(chunks):
                part = slice(index * CHUNK, (index + 1) * CHUNK)
                r.total[:, :, part] = turned_dot(
                    r.kept[part, hidden:], r.given_v[...].reshape(micros * rows, upper), micros
                )
                if index % 2:
                    span = pl.ds((index - 1) * CHUNK, 2 * CHUNK)
                    sem = r.sems.at[1 + index // 2]
                    writes.append(pltpu.make_async_copy(r.total.at[:, :, span], r.out.at[:, :, span], sem))
                    writes[-1].start()
            for write in writes:
                write.wait()

    shape = ((micros, rows, hidden), jnp.float32)
    return kernel(
        "upper_product", body, dict(lengths=lengths, kept=kept, given=given), dict(out=shape),
        dict(given_v=(given.shape, jnp.bfloat16), total=shape),
        1 + chunks // 2, near=("kept",), flops=1_600_000_000, moved=3_000_000, limit=TIGHT,
    )["out"]


def coefficients(message, hidden, count):
    found = []
    for far in range(count):
        coef = jnp.zeros((message.shape[0], 1), jnp.float32)
        for part in reversed(range(PARTS)):
            at = hidden + far * PARTS + part
            coef = coef + message[:, at : at + 1].astype(jnp.float32)
        found.append(coef)
    return found


def rebuild(above, raw, ups, coefs, hidden):
    high = raw[:, hidden:]
    for far in reversed(range(len(coefs))):
        value = (high.astype(jnp.float32) - ups[far][...].astype(jnp.float32) * coefs[far]).astype(jnp.bfloat16)
        high = jnp.where(above > far, value, high)
    raw[:, hidden:] = high


def cut(length, raw, tiles):
    rows, width = raw.shape
    keep = lax.broadcasted_iota(jnp.int32, (rows, HEAD), 0) < length
    for tile in range(width // HEAD):
        value = raw[:, tile * HEAD : (tile + 1) * HEAD].astype(jnp.float32)
        tiles[tile] = jnp.where(keep, value, 0.0).astype(jnp.bfloat16)


def layer_step(step, lengths, weight, resident, state, incoming, xups, uppers, gain_acc, store, masked, last):
    micros, rows, width = state["inputs"].shape
    hidden = weight.shape[0]
    heads = hidden // HEAD
    chunks = hidden // CHUNK
    count = len(xups)
    scale = SCORE_FACTOR / math.sqrt(HEAD)

    operands = dict(
        lengths=lengths, weight=weight, **state, gacc=gain_acc, store_in=store, xups=list(xups), uppers=list(uppers)
    )
    aliases = ["store"]
    outs = dict(gout=((1, hidden), jnp.float32), store=(store.shape, store.dtype))
    near = ["gain", "gacc", "gout", "inc", "message"] + (["weight"] if resident else [])
    half = ((rows, hidden), jnp.bfloat16)
    half_float = ((rows, hidden), jnp.float32)
    full = ((rows, width), jnp.bfloat16)
    scratch = dict(
        raw=full, sums=half_float, base_v=half_float, shared_v=half, probs_v=((heads, rows, rows), jnp.float32),
        turned_v=((heads, rows, rows), jnp.bfloat16), inv_v=((rows, HEAD), jnp.float32), x_v=full,
        scaled=half_float, grad=full, ups_v=[half] * count, uppers_v=[half_float] * count,
    )
    if not resident:
        scratch["block"] = ((chunks, CHUNK, hidden), jnp.bfloat16)
    if masked is not None:
        operands["masked_in"] = masked
        outs["masked"] = (masked.shape, masked.dtype)
        scratch["tiles"] = ((width // HEAD, rows, HEAD), jnp.bfloat16)
        aliases.append("masked")
    if incoming is not None:
        operands["inc"] = incoming
    if not last:
        outs["message"] = ((rows, hidden + HEAD), jnp.bfloat16)

    def body(r):
        active, micro, above = place(step, micros)
        used = []

        def copy(source, target):
            made = pltpu.make_async_copy(source, target, r.sems.at[len(used)])
            used.append(made)
            return made

        def guarded(far, action):
            @pl.when(above > far)
            def _():
                action()

        @pl.when(jnp.logical_not(active))
        def _():
            r.gout[...] = r.gacc[...]

        @pl.when(active)
        def _():
            cot = copy(r.cot.at[micro], r.raw)
            cot.start()
            if not resident:
                blocks = []
                for index in range(chunks):
                    source = r.weight.at[pl.ds(index * CHUNK, CHUNK), pl.ds(0, hidden)]
                    blocks.append(copy(source, r.block.at[index]))
                for block in blocks[:WINDOW]:
                    block.start()
            pairs = [(r.base, r.base_v), (r.probs, r.probs_v), (r.shared, r.shared_v), (r.turned, r.turned_v),
                     (r.inv, r.inv_v), (r.inputs, r.x_v)]
            rest = [copy(source.at[micro], target) for source, target in pairs]
            extra = [copy(r.uppers[far].at[micro], r.uppers_v[far]) for far in range(count)]
            ups = [copy(r.xups[far].at[micro], r.ups_v[far]) for far in range(count)]

            def start_rest():
                for made in rest:
                    made.start()
                for far in range(count):
                    guarded(far, extra[far].start)
                    guarded(far, ups[far].start)

            if resident:
                start_rest()
            cot.wait()
            coefs = []
            if incoming is not None:
                @pl.when(above > 0)
                def _():
                    r.raw[:, :hidden] = r.inc[:, :hidden]

                coefs = coefficients(r.inc[...], hidden, count)
            for index in range(chunks):
                part = slice(index * CHUNK, (index + 1) * CHUNK)
                if resident:
                    block = r.weight[part, :hidden]
                else:
                    blocks[index].wait()
                    if index + WINDOW < chunks:
                        blocks[index + WINDOW].start()
                    elif index + WINDOW == chunks:
                        start_rest()
                    block = r.block[index]
                r.sums[:, part] = dot_nt(block, r.raw[:, :hidden]).T
            for made in rest:
                made.wait()
            for far in range(count):
                @pl.when(above > far)
                def _():
                    extra[far].wait()
                    r.base_v[...] = r.base_v[...] - coefs[far] * r.uppers_v[far][...]

            length = r.lengths[0, micro]
            keep = lax.broadcasted_iota(jnp.int32, (rows, HEAD), 0) < length
            inv = r.inv_v[...]
            inner = jnp.zeros((rows, HEAD), jnp.float32)
            for head in range(heads):
                cols = slice(head * HEAD, (head + 1) * HEAD)
                shared = r.shared_v[:, cols]
                probs = r.probs_v[head]
                grad_head = jnp.where(keep, r.sums[:, cols] + r.base_v[:, cols], 0.0).astype(jnp.bfloat16)
                grad_probs = dot_nt(grad_head, shared)
                delta = jnp.sum(probs * grad_probs, axis=1, keepdims=True)
                dscore = scale * probs * (grad_probs - delta)
                left = jnp.concatenate([(dscore + dscore.T).astype(jnp.bfloat16), r.turned_v[head]], axis=1)
                grad_shared = dot_nn(left, jnp.concatenate([shared, grad_head], axis=0))
                x_head = r.x_v[:, cols].astype(jnp.float32)
                gain_term = jnp.sum(grad_shared * (x_head * inv), axis=0, keepdims=True)
                r.gout[:, cols] = r.gacc[:, cols] + gain_term
                scaled = grad_shared * r.gain[:, cols]
                inner = inner + scaled * x_head
                r.scaled[:, cols] = scaled
            inv = inv[:, :1]
            coef = inv * inv * inv * (jnp.sum(inner, axis=1, keepdims=True) / width)
            low = r.raw[:, :hidden].astype(jnp.float32) + inv * r.scaled[...]
            low = (low - r.x_v[:, :hidden].astype(jnp.float32) * coef).astype(jnp.bfloat16)
            r.grad[:, :hidden] = low
            if not last:
                r.message[:, :hidden] = low
                lane = lax.broadcasted_iota(jnp.int32, (rows, HEAD), 1)
                if incoming is None:
                    tail = jnp.zeros((rows, HEAD), jnp.float32)
                else:
                    came = jnp.where(above == 0, 0.0, r.inc[:, hidden:].astype(jnp.float32))
                    tail = jnp.where(lane < PARTS, 0.0, pltpu.roll(came, PARTS, axis=1))
                left_over = coef
                for part in range(PARTS):
                    piece = left_over.astype(jnp.bfloat16).astype(jnp.float32)
                    tail = jnp.where(lane == part, piece, tail)
                    left_over = left_over - piece
                r.message[:, hidden:] = tail.astype(jnp.bfloat16)
            for far in range(count):
                guarded(far, ups[far].wait)
            rebuild(above, r.raw, r.ups_v, coefs, hidden)
            high = r.raw[:, hidden:].astype(jnp.float32) - r.x_v[:, hidden:].astype(jnp.float32) * coef
            r.grad[:, hidden:] = high.astype(jnp.bfloat16)
            keepers = [copy(r.grad, r.store.at[micro])]
            keepers[0].start()
            if masked is not None:
                cut(length, r.raw, r.tiles)
                keepers.append(copy(r.tiles, r.masked.at[:, micro]))
                keepers[1].start()
            for made in keepers:
                made.wait()

    return kernel(
        "layer_step", body, operands, outs, scratch, chunks + 2 * count + 12, aliases,
        near=near, flops=3_000_000_000, moved=14_000_000, limit=TIGHT if resident else LIMIT,
    )


def receive_step(step, lengths, cot, incoming, xups, masked):
    micros, rows, width = cot.shape
    hidden = incoming.shape[1] - HEAD
    count = len(xups)

    def body(r):
        active, micro, above = place(step, micros)

        @pl.when(active)
        def _():
            loads = [pltpu.make_async_copy(r.cot.at[micro], r.raw, r.sems.at[1])]
            for far in range(count):
                loads.append(pltpu.make_async_copy(r.xups[far].at[micro], r.ups_v[far], r.sems.at[2 + far]))
            for load in loads:
                load.start()
            for load in loads:
                load.wait()

            @pl.when(above > 0)
            def _():
                r.raw[:, :hidden] = r.inc[:, :hidden]

            rebuild(above, r.raw, r.ups_v, coefficients(r.inc[...], hidden, count), hidden)
            cut(r.lengths[0, micro], r.raw, r.tiles)
            write = pltpu.make_async_copy(r.tiles, r.masked.at[:, micro], r.sems.at[0])
            write.start()
            write.wait()

    return kernel(
        "receive_step", body, dict(lengths=lengths, cot=cot, inc=incoming, masked_in=masked, xups=list(xups)),
        dict(masked=(masked.shape, masked.dtype)),
        dict(
            raw=((rows, width), jnp.bfloat16), tiles=((width // HEAD, rows, HEAD), jnp.bfloat16),
            ups_v=[((rows, width - hidden), jnp.bfloat16)] * count,
        ),
        2 + count, ["masked"], near=("inc",), flops=1_000_000, moved=2_000_000,
    )["masked"]


def buffers(lengths, **shapes):
    outs = {key: (shape, jnp.bfloat16) for key, shape in shapes.items()}
    return kernel("buffers", lambda r: None, dict(lengths=lengths), outs, {}, 1)


def product(attended, columns, gain, owners):
    depth, hidden = attended.shape
    own = hidden // owners

    def body(att_ref, col_ref, gain_ref, out_ref, acc):
        @pl.when(pl.program_id(0) == 0)
        def _():
            acc[...] = jnp.zeros_like(acc)

        acc[...] += dot_tn(col_ref[...], att_ref[...])

        @pl.when(pl.program_id(0) == pl.num_programs(0) - 1)
        def _():
            for pair in range(owners // 2):
                cols = slice(pair * 2 * own, (pair + 1) * 2 * own)
                turned = acc[:, cols].T.astype(jnp.bfloat16)
                gains = jnp.broadcast_to(gain_ref[:, cols], (PAD - own, HEAD)).astype(jnp.bfloat16)
                for side in range(2):
                    out_ref[2 * pair + side, :own] = turned[side * own : (side + 1) * own]
                    out_ref[2 * pair + side, own:] = gains

    return pl.pallas_call(
        body,
        name="product",
        grid=(depth // DEPTH,),
        in_specs=[
            pl.BlockSpec((DEPTH, hidden), lambda i: (i, 0)),
            pl.BlockSpec((DEPTH, HEAD), lambda i: (i, 0)),
            pl.BlockSpec((1, hidden), lambda i: (0, 0)),
        ],
        out_specs=pl.BlockSpec((owners, PAD, HEAD), lambda i: (0, 0, 0)),
        out_shape=jax.ShapeDtypeStruct((owners, PAD, HEAD), jnp.bfloat16),
        scratch_shapes=[pltpu.VMEM((HEAD, hidden), jnp.float32)],
        compiler_params=pltpu.CompilerParams(vmem_limit_bytes=40 << 20),
        cost_estimate=pl.CostEstimate(
            flops=2 * depth * hidden * HEAD, bytes_accessed=2 * depth * hidden, transcendentals=0
        ),
    )(attended, columns, gain)


def unpack(block, own):
    sources = block.shape[0]

    def body(block_ref, proj_ref, gain_ref):
        total = jnp.zeros((1, HEAD), jnp.float32)
        for source in range(sources):
            proj_ref[:, source * HEAD : (source + 1) * HEAD] = block_ref[source, :own].astype(jnp.float32)
            total = total + block_ref[source, own : own + 16].astype(jnp.float32)[:1]
        odd = lax.rem(lax.axis_index(DP), 2) == 1
        gain_ref[...] = jnp.where(odd, total[:, own:], total[:, :own])

    return pl.pallas_call(
        body,
        name="unpack",
        in_specs=[VMEM],
        out_specs=[VMEM] * 2,
        out_shape=[
            jax.ShapeDtypeStruct((own, sources * HEAD), jnp.float32),
            jax.ShapeDtypeStruct((1, own), jnp.float32),
        ],
        compiler_params=pltpu.CompilerParams(vmem_limit_bytes=LIMIT),
    )(block)


def per_device(saved_inputs, cotangent, out_proj, norm_gain, lengths):
    sections = lax.axis_size("section")
    replicas = lax.axis_size(DP)
    inputs = saved_inputs[0, 0]
    cot = cotangent[0]
    weight = out_proj[0]
    micros, rows, width = inputs.shape
    hidden = weight.shape[0]
    tiles = width // HEAD

    first = prelude(lengths, inputs, norm_gain)
    attended = first.pop("attended").reshape(micros * rows, hidden)
    own_up = first.pop("upper")
    round_once = lax.ppermute(own_up, "section", [(3, 0), (2, 3)])
    near = lax.ppermute(own_up, "section", [(3, 2), (2, 1), (1, 0)])
    round_twice = lax.ppermute(round_once, "section", [(0, 1), (3, 0)])
    xups = [near, round_twice, round_once]
    gathered = lax.all_gather(attended, DP, axis=0, tiled=True)

    kept = buffers(lengths, store=(micros, rows, width), masked=(tiles, micros, rows, HEAD))
    store, masked = kept["store"], kept["masked"]
    loaded = load_weight(lengths, weight, cot)
    state = dict(inputs=inputs, cot=cot, base=loaded["base"], gain=norm_gain, **first)
    gain_acc = jnp.zeros((1, hidden), jnp.float32)

    steps = SKEW * (sections - 1) + micros
    arriving = {}
    uppers = []
    for step in range(steps):
        incoming = arriving.get(step)
        last = step == steps - 1
        depth = min(step // SKEW, sections - 1)
        while len(uppers) < depth:
            uppers.append(upper_product(lengths, loaded["kept"], xups[len(uppers)], len(uppers) + 1))
        if last:
            masked = receive_step(step, lengths, cot, incoming, xups, masked)
            columns = lax.all_to_all(masked.reshape(tiles, micros * rows, HEAD), DP, 0, 0, tiled=True)
        done = layer_step(
            step, lengths, weight if last else loaded["kept"], not last, state, incoming, xups[:depth], uppers,
            gain_acc, store, None if last else masked, last,
        )
        gain_acc, store = done["gout"], done["store"]
        if last:
            break
        masked = done["masked"]
        route = [
            (src, src - 1)
            for src in range(1, sections)
            if 0 <= step - SKEW * (sections - 1 - src) < micros
        ]
        if route:
            arriving[step + SKEW] = lax.ppermute(done["message"], "section", route)

    packed = product(gathered, columns.reshape(replicas * micros * rows, HEAD), gain_acc, replicas)
    block = lax.all_to_all(packed, DP, 0, 0, tiled=True)
    proj, gain = unpack(block, hidden // replicas)
    return (store[None, None], proj[None], gain)


def solution(mesh):
    placed = (
        P("section", "dp", None, None, None),
        P("dp", None, None, None),
        P("section", None, None),
        P("section", None),
        P("dp", None),
    )
    return jax.shard_map(
        per_device,
        mesh=mesh,
        in_specs=placed,
        out_specs=(
            P("section", "dp", None, None, None),
            P("section", "dp", None),
            P("section", "dp"),
        ),
        check_vma=False,
    )
```

```python
import math
from types import SimpleNamespace

import jax
import jax.numpy as jnp
from jax import lax
from jax.experimental import pallas as pl
from jax.experimental.pallas import tpu as pltpu
from jax.sharding import Mesh
from jax.sharding import PartitionSpec as P

HEAD = 128
NORM_EPS = 1e-06
SCORE_FACTOR = 0.6
MASKED_SCORE = -1e30
RING = ("x", "core")
PLANE = ("x", "y", "core")
SKEW = 2
CHUNK = 256
LIMIT = 56 << 20
TIGHT = 10 << 20
WINDOW = 2
PARTS = 3
EXTRA = 16


VMEM = pl.BlockSpec(memory_space=pltpu.VMEM)
SMEM = pl.BlockSpec(memory_space=pltpu.SMEM)
FAR = pl.BlockSpec(memory_space=pltpu.HBM)


def dot_nt(a, b):
    return lax.dot_general(a, b, (((1,), (1,)), ((), ())), preferred_element_type=jnp.float32)


def dot_nn(a, b):
    return lax.dot_general(a, b, (((1,), (0,)), ((), ())), preferred_element_type=jnp.float32)


def dot_tn(a, b):
    return lax.dot_general(a, b, (((0,), (0,)), ((), ())), preferred_element_type=jnp.float32)


def kernel(name, body, operands, outs, scratch, sems, aliases=(), near=(), flops=0, moved=0, limit=LIMIT):
    sizes = {key: len(value) for key, value in (*operands.items(), *scratch.items()) if isinstance(value, list)}

    def flat(items):
        return [one for value in items.values() for one in (value if isinstance(value, list) else [value])]

    def run(*refs):
        refs = iter(refs)
        named = {}
        for key in (*operands, *outs, *scratch):
            named[key] = [next(refs) for _ in range(sizes[key])] if key in sizes else next(refs)
        body(SimpleNamespace(**named, sems=next(refs)))

    order = {key: sum(sizes.get(k, 1) for k in list(operands)[:i]) for i, key in enumerate(operands)}
    in_specs = []
    for key in operands:
        in_specs += [SMEM if key == "lengths" else VMEM if key in near else FAR] * sizes.get(key, 1)
    values = pl.pallas_call(
        run,
        name=name,
        in_specs=in_specs,
        out_specs=[VMEM if key in near else FAR for key in outs],
        out_shape=[jax.ShapeDtypeStruct(*item) for item in outs.values()],
        scratch_shapes=[pltpu.VMEM(*item) for item in flat(scratch)] + [pltpu.SemaphoreType.DMA((sems,))],
        input_output_aliases={order[key + "_in"]: list(outs).index(key) for key in aliases},
        compiler_params=pltpu.CompilerParams(vmem_limit_bytes=limit),
        cost_estimate=pl.CostEstimate(flops=flops, bytes_accessed=moved, transcendentals=0),
    )(*flat(operands))
    return dict(zip(outs, values))


def prelude(lengths, inputs, gain):
    micros, rows, width = inputs.shape
    hidden = gain.shape[1]
    heads = hidden // HEAD
    scale = SCORE_FACTOR / math.sqrt(HEAD)

    def body(r):
        loads = [
            pltpu.make_async_copy(r.inputs.at[micro], r.x.at[micro], r.sems.at[micro]) for micro in range(micros)
        ]
        for load in loads:
            load.start()
        writes = [pltpu.make_async_copy(r.x.at[:, :, pl.ds(hidden, width - hidden)], r.upper, r.sems.at[micros])]
        for load in loads:
            load.wait()
        writes[0].start()
        for micro in range(micros):
            x = r.x[micro].astype(jnp.float32)
            inv = lax.rsqrt(jnp.mean(x * x, axis=1, keepdims=True) + NORM_EPS)
            r.inv_v[micro] = jnp.broadcast_to(inv, (rows, HEAD))
            r.shared_v[micro] = (x[:, :hidden] * inv * r.gain[...]).astype(jnp.bfloat16)
            live = lax.broadcasted_iota(jnp.int32, (rows, rows), 1) < r.lengths[0, micro]
            for head in range(heads):
                cols = slice(head * HEAD, (head + 1) * HEAD)
                shared = r.shared_v[micro, :, cols]
                scores = jnp.where(live, dot_nt(shared, shared) * scale, MASKED_SCORE)
                exponent = jnp.exp(scores - jnp.max(scores, axis=1, keepdims=True))
                probs = exponent / jnp.sum(exponent, axis=1, keepdims=True)
                r.probs_v[micro, head] = probs
                r.turned_v[micro, head] = probs.T.astype(jnp.bfloat16)
                r.attended_v[micro, :, cols] = dot_nn(probs.astype(jnp.bfloat16), shared).astype(jnp.bfloat16)
            pairs = [
                (r.attended_v, r.attended), (r.shared_v, r.shared), (r.probs_v, r.probs), (r.turned_v, r.turned),
                (r.inv_v, r.inv),
            ]
            for index, (source, target) in enumerate(pairs):
                sem = r.sems.at[micros + 1 + len(pairs) * micro + index]
                writes.append(pltpu.make_async_copy(source.at[micro], target.at[micro], sem))
                writes[-1].start()
        for write in writes:
            write.wait()

    wide = ((micros, rows, hidden), jnp.bfloat16)
    square = (micros, heads, rows, rows)
    outs = dict(
        attended=wide, shared=wide, probs=(square, jnp.float32), turned=(square, jnp.bfloat16),
        inv=((micros, rows, HEAD), jnp.float32), upper=((micros, rows, width - hidden), jnp.bfloat16),
    )
    scratch = dict(
        x=(inputs.shape, jnp.bfloat16), attended_v=wide, shared_v=wide, probs_v=outs["probs"],
        turned_v=outs["turned"], inv_v=outs["inv"],
    )
    return kernel(
        "prelude", body, dict(lengths=lengths, inputs=inputs, gain=gain), outs, scratch,
        6 * micros + 1, near=("gain",), flops=500_000_000, moved=8_000_000, limit=TIGHT,
    )


def place(step, micros):
    above = lax.axis_size("section") - 1 - lax.axis_index("section")
    micro = step - SKEW * above
    active = jnp.logical_and(micro >= 0, micro < micros)
    return active, jnp.clip(micro, 0, micros - 1), above


def turned_dot(weight, rows_from, micros):
    turned = dot_nt(weight, rows_from).T
    return turned.reshape(micros, turned.shape[0] // micros, turned.shape[1])


def upper_product(lengths, kept, given, least):
    hidden, width = kept.shape
    micros, rows, wide = given.shape
    upper = width - hidden
    chunks = hidden // CHUNK

    def body(r):
        above = lax.axis_size("section") - 1 - lax.axis_index("section")

        @pl.when(above >= least)
        def _():
            load = pltpu.make_async_copy(r.given.at[:, :, pl.ds(wide - upper, upper)], r.given_v, r.sems.at[0])
            load.start()
            load.wait()
            writes = []
            for index in range(chunks):
                part = slice(index * CHUNK, (index + 1) * CHUNK)
                r.total[:, :, part] = turned_dot(
                    r.kept[part, hidden:], r.given_v[...].reshape(micros * rows, upper), micros
                )
                if index % 2:
                    span = pl.ds((index - 1) * CHUNK, 2 * CHUNK)
                    sem = r.sems.at[1 + index // 2]
                    writes.append(pltpu.make_async_copy(r.total.at[:, :, span], r.out.at[:, :, span], sem))
                    writes[-1].start()
            for write in writes:
                write.wait()

    shape = ((micros, rows, hidden), jnp.float32)
    return kernel(
        "upper_product", body, dict(lengths=lengths, kept=kept, given=given), dict(out=shape),
        dict(given_v=((micros, rows, upper), jnp.bfloat16), total=shape),
        1 + chunks // 2, near=("kept",), flops=1_600_000_000, moved=3_000_000, limit=TIGHT,
    )["out"]


def coefficients(message, hidden, count):
    found = []
    for far in range(count):
        coef = jnp.zeros((message.shape[0], 1), jnp.float32)
        for part in reversed(range(PARTS)):
            at = hidden + far * PARTS + part
            coef = coef + message[:, at : at + 1].astype(jnp.float32)
        found.append(coef)
    return found


def rebuild(above, raw, ups, coefs, hidden):
    high = raw[:, hidden:]
    for far in reversed(range(len(coefs))):
        value = (high.astype(jnp.float32) - ups[far][...].astype(jnp.float32) * coefs[far]).astype(jnp.bfloat16)
        high = jnp.where(above > far, value, high)
    raw[:, hidden:] = high


def cut(length, raw, tiles):
    rows, width = raw.shape
    keep = lax.broadcasted_iota(jnp.int32, (rows, HEAD), 0) < length
    wide = tiles.shape[2]
    for tile in range(width // HEAD):
        value = raw[:, tile * HEAD : (tile + 1) * HEAD].astype(jnp.float32)
        index, at = divmod(tile * HEAD, wide)
        tiles[index, :, at : at + HEAD] = jnp.where(keep, value, 0.0).astype(jnp.bfloat16)


def layer_step(step, lengths, weight, resident, state, incoming, xups, uppers, gain_acc, store, masked, last):
    micros, rows, width = state["inputs"].shape
    hidden = weight.shape[0]
    heads = hidden // HEAD
    chunks = hidden // CHUNK
    count = len(xups)
    scale = SCORE_FACTOR / math.sqrt(HEAD)

    operands = dict(
        lengths=lengths, weight=weight, **state, gacc=gain_acc, store_in=store, xups=list(xups), uppers=list(uppers)
    )
    aliases = ["store"]
    outs = dict(gout=((1, hidden), jnp.float32), store=(store.shape, store.dtype))
    near = ["gain", "gacc", "gout", "inc", "message"] + (["weight"] if resident else [])
    half = ((rows, hidden), jnp.bfloat16)
    half_float = ((rows, hidden), jnp.float32)
    full = ((rows, width), jnp.bfloat16)
    scratch = dict(
        raw=full, sums=half_float, base_v=half_float, shared_v=half, probs_v=((heads, rows, rows), jnp.float32),
        turned_v=((heads, rows, rows), jnp.bfloat16), inv_v=((rows, HEAD), jnp.float32), x_v=full,
        scaled=half_float, grad=full, ups_v=[half] * count, uppers_v=[half_float] * count,
    )
    if not resident:
        scratch["block"] = ((chunks, CHUNK, hidden), jnp.bfloat16)
    if masked is not None:
        operands["masked_in"] = masked
        outs["masked"] = (masked.shape, masked.dtype)
        scratch["tiles"] = ((masked.shape[0], rows, masked.shape[3]), jnp.bfloat16)
        aliases.append("masked")
    if incoming is not None:
        operands["inc"] = incoming
    if not last:
        outs["message"] = ((rows, hidden + HEAD), jnp.bfloat16)

    def body(r):
        active, micro, above = place(step, micros)
        used = []

        def copy(source, target):
            made = pltpu.make_async_copy(source, target, r.sems.at[len(used)])
            used.append(made)
            return made

        def guarded(far, action):
            @pl.when(above > far)
            def _():
                action()

        @pl.when(jnp.logical_not(active))
        def _():
            r.gout[...] = r.gacc[...]

        @pl.when(active)
        def _():
            cot = copy(r.cot.at[micro], r.raw)
            cot.start()
            if not resident:
                blocks = []
                for index in range(chunks):
                    source = r.weight.at[pl.ds(index * CHUNK, CHUNK), pl.ds(0, hidden)]
                    blocks.append(copy(source, r.block.at[index]))
                for block in blocks[:WINDOW]:
                    block.start()
            pairs = [(r.base, r.base_v), (r.probs, r.probs_v), (r.shared, r.shared_v), (r.turned, r.turned_v),
                     (r.inv, r.inv_v), (r.inputs, r.x_v)]
            rest = [copy(source.at[micro], target) for source, target in pairs]
            extra = [copy(r.uppers[far].at[micro], r.uppers_v[far]) for far in range(count)]
            ups = [copy(r.xups[far].at[micro], r.ups_v[far]) for far in range(count)]

            def start_rest():
                for made in rest:
                    made.start()
                for far in range(count):
                    guarded(far, extra[far].start)
                    guarded(far, ups[far].start)

            if resident:
                start_rest()
            cot.wait()
            coefs = []
            if incoming is not None:
                @pl.when(above > 0)
                def _():
                    r.raw[:, :hidden] = r.inc[:, :hidden]

                coefs = coefficients(r.inc[...], hidden, count)
            for index in range(chunks):
                part = slice(index * CHUNK, (index + 1) * CHUNK)
                if resident:
                    block = r.weight[part, :hidden]
                else:
                    blocks[index].wait()
                    if index + WINDOW < chunks:
                        blocks[index + WINDOW].start()
                    elif index + WINDOW == chunks:
                        start_rest()
                    block = r.block[index]
                r.sums[:, part] = dot_nt(block, r.raw[:, :hidden]).T
            for made in rest:
                made.wait()
            for far in range(count):
                @pl.when(above > far)
                def _():
                    extra[far].wait()
                    r.base_v[...] = r.base_v[...] - coefs[far] * r.uppers_v[far][...]

            length = r.lengths[0, micro]
            keep = lax.broadcasted_iota(jnp.int32, (rows, HEAD), 0) < length
            inv = r.inv_v[...]
            inner = jnp.zeros((rows, HEAD), jnp.float32)
            for head in range(heads):
                cols = slice(head * HEAD, (head + 1) * HEAD)
                shared = r.shared_v[:, cols]
                probs = r.probs_v[head]
                grad_head = jnp.where(keep, r.sums[:, cols] + r.base_v[:, cols], 0.0).astype(jnp.bfloat16)
                grad_probs = dot_nt(grad_head, shared)
                delta = jnp.sum(probs * grad_probs, axis=1, keepdims=True)
                dscore = scale * probs * (grad_probs - delta)
                left = jnp.concatenate([(dscore + dscore.T).astype(jnp.bfloat16), r.turned_v[head]], axis=1)
                grad_shared = dot_nn(left, jnp.concatenate([shared, grad_head], axis=0))
                x_head = r.x_v[:, cols].astype(jnp.float32)
                gain_term = jnp.sum(grad_shared * (x_head * inv), axis=0, keepdims=True)
                r.gout[:, cols] = r.gacc[:, cols] + gain_term
                scaled = grad_shared * r.gain[:, cols]
                inner = inner + scaled * x_head
                r.scaled[:, cols] = scaled
            inv = inv[:, :1]
            coef = inv * inv * inv * (jnp.sum(inner, axis=1, keepdims=True) / width)
            low = r.raw[:, :hidden].astype(jnp.float32) + inv * r.scaled[...]
            low = (low - r.x_v[:, :hidden].astype(jnp.float32) * coef).astype(jnp.bfloat16)
            r.grad[:, :hidden] = low
            if not last:
                r.message[:, :hidden] = low
                lane = lax.broadcasted_iota(jnp.int32, (rows, HEAD), 1)
                if incoming is None:
                    tail = jnp.zeros((rows, HEAD), jnp.float32)
                else:
                    came = jnp.where(above == 0, 0.0, r.inc[:, hidden:].astype(jnp.float32))
                    tail = jnp.where(lane < PARTS, 0.0, pltpu.roll(came, PARTS, axis=1))
                left_over = coef
                for part in range(PARTS):
                    piece = left_over.astype(jnp.bfloat16).astype(jnp.float32)
                    tail = jnp.where(lane == part, piece, tail)
                    left_over = left_over - piece
                r.message[:, hidden:] = tail.astype(jnp.bfloat16)
            for far in range(count):
                guarded(far, ups[far].wait)
            rebuild(above, r.raw, r.ups_v, coefs, hidden)
            high = r.raw[:, hidden:].astype(jnp.float32) - r.x_v[:, hidden:].astype(jnp.float32) * coef
            r.grad[:, hidden:] = high.astype(jnp.bfloat16)
            keepers = [copy(r.grad, r.store.at[micro])]
            keepers[0].start()
            if masked is not None:
                cut(length, r.raw, r.tiles)
                keepers.append(copy(r.tiles, r.masked.at[:, micro]))
                keepers[1].start()
            for made in keepers:
                made.wait()

    return kernel(
        "layer_step", body, operands, outs, scratch, chunks + 2 * count + 12, aliases,
        near=near, flops=3_000_000_000, moved=14_000_000, limit=TIGHT if resident else LIMIT,
    )


def receive_step(step, lengths, cot, incoming, xups, masked):
    micros, rows, width = cot.shape
    hidden = incoming.shape[1] - HEAD
    count = len(xups)

    def body(r):
        active, micro, above = place(step, micros)

        @pl.when(active)
        def _():
            loads = [pltpu.make_async_copy(r.cot.at[micro], r.raw, r.sems.at[1])]
            for far in range(count):
                loads.append(pltpu.make_async_copy(r.xups[far].at[micro], r.ups_v[far], r.sems.at[2 + far]))
            for load in loads:
                load.start()
            for load in loads:
                load.wait()

            @pl.when(above > 0)
            def _():
                r.raw[:, :hidden] = r.inc[:, :hidden]

            rebuild(above, r.raw, r.ups_v, coefficients(r.inc[...], hidden, count), hidden)
            cut(r.lengths[0, micro], r.raw, r.tiles)
            write = pltpu.make_async_copy(r.tiles, r.masked.at[:, micro], r.sems.at[0])
            write.start()
            write.wait()

    return kernel(
        "receive_step", body, dict(lengths=lengths, cot=cot, inc=incoming, masked_in=masked, xups=list(xups)),
        dict(masked=(masked.shape, masked.dtype)),
        dict(
            raw=((rows, width), jnp.bfloat16), tiles=((masked.shape[0], rows, masked.shape[3]), jnp.bfloat16),
            ups_v=[((rows, width - hidden), jnp.bfloat16)] * count,
        ),
        2 + count, ["masked"], near=("inc",), flops=1_000_000, moved=2_000_000, limit=TIGHT,
    )["masked"]


def buffers(lengths, **shapes):
    outs = {key: (shape, jnp.bfloat16) for key, shape in shapes.items()}
    return kernel("buffers", lambda r: None, dict(lengths=lengths), outs, {}, 1, limit=1 << 20)


def product(lengths, mine, theirs, columns, gain, owners):
    depth, hidden = mine[0].shape
    members, _, wide = columns.shape
    own = hidden // owners
    turns = members // 2
    rows = own * wide // HEAD + EXTRA

    def body(r):
        place_x = lax.axis_index("x")
        core = lax.axis_index("core")
        loads = []
        for turn in range(turns):
            behind = lax.rem(place_x - turn + turns, turns)
            for side, pieces in enumerate((r.mine, r.theirs)):
                member = behind * 2 + (core if side == 0 else 1 - core)
                made = pltpu.make_async_copy(pieces[turn], r.stack.at[member], r.sems.at[2 * turn + side])
                made.start()
                loads.append(made)
        for member in range(members):
            r.turned[:, member * depth : (member + 1) * depth] = r.columns[member].T
        for made in loads:
            made.wait()
        span = 2 * CHUNK
        for start in range(0, hidden, span):
            right = r.stack[:, :, start : start + span].reshape(members * depth, span)
            sums = dot_nn(r.turned[...], right)
            for owner in range(start // own, (start + span) // own, 2):
                at = owner * own - start
                gains = jnp.broadcast_to(r.gain[:, owner * own : (owner + 2) * own], (EXTRA, HEAD))
                for tile in range(wide // HEAD):
                    block = sums[tile * HEAD : (tile + 1) * HEAD, at : at + HEAD].T.astype(jnp.bfloat16)
                    for side in range(2):
                        r.out[owner + side, tile * own : (tile + 1) * own] = block[side * own : (side + 1) * own]
                for side in range(2):
                    r.out[owner + side, rows - EXTRA :] = gains.astype(jnp.bfloat16)

    return kernel(
        "product", body,
        dict(lengths=lengths, mine=list(mine), theirs=list(theirs), columns=columns, gain=gain),
        dict(out=((owners, rows, HEAD), jnp.bfloat16)),
        dict(
            stack=((members, depth, hidden), jnp.bfloat16), turned=((wide, members * depth), jnp.bfloat16),
        ),
        members, near=("columns", "gain", "out"), flops=2 * members * depth * hidden * wide,
        moved=2 * members * depth * (hidden + wide), limit=LIMIT,
    )["out"]


def unpack(block, own, width):
    sources, rows, _ = block.shape
    wide = (rows - EXTRA) // own * HEAD

    def body(block_ref, proj_ref, gain_ref):
        rings = lax.axis_size("y")
        total = jnp.zeros((EXTRA, HEAD), jnp.float32)
        for member in range(width // wide):
            place_x, core = divmod(member, 2)
            froms = [(place_x * rings + ring) * 2 + core for ring in range(rings)]
            for tile in range(wide // HEAD):
                value = jnp.zeros((own, HEAD), jnp.float32)
                for source in froms:
                    value = value + block_ref[source, tile * own : (tile + 1) * own].astype(jnp.float32)
                at = member * wide + tile * HEAD
                proj_ref[:, at : at + HEAD] = value
            for source in froms:
                total = total + block_ref[source, rows - EXTRA :].astype(jnp.float32)
        odd = lax.axis_index("core") == 1
        gain_ref[...] = jnp.where(odd, total[:1, own:], total[:1, :own])

    return pl.pallas_call(
        body,
        name="unpack",
        in_specs=[VMEM],
        out_specs=[VMEM] * 2,
        out_shape=[
            jax.ShapeDtypeStruct((own, width), jnp.float32),
            jax.ShapeDtypeStruct((1, own), jnp.float32),
        ],
        compiler_params=pltpu.CompilerParams(vmem_limit_bytes=TIGHT),
    )(block)


def per_device(saved_inputs, cotangent, out_proj, norm_gain, lengths):
    sections = lax.axis_size("section")
    replicas = lax.axis_size(PLANE)
    members = lax.axis_size(RING)
    inputs = saved_inputs[0, 0]
    cot = cotangent[0]
    weight = out_proj[0]
    micros, rows, width = inputs.shape
    hidden = weight.shape[0]

    first = prelude(lengths, inputs, norm_gain)
    attended = first.pop("attended").reshape(micros * rows, hidden)
    own_up = first.pop("upper")
    round_once = lax.ppermute(own_up, "section", [(3, 0), (2, 3)])
    near = lax.ppermute(own_up, "section", [(3, 2), (2, 1), (1, 0)])
    round_twice = lax.ppermute(round_once, "section", [(0, 1), (3, 0)])
    xups = [near, round_twice, round_once]
    turns = lax.axis_size("x")
    ahead = [(i, (i + 1) % turns) for i in range(turns)]
    back = [((i + 1) % turns, i) for i in range(turns)]
    one = lax.ppermute(attended, "x", ahead)
    three = lax.ppermute(attended, "x", back)
    two = lax.ppermute(one, "x", ahead)
    mine = [attended, one, two, three]
    theirs = [lax.ppermute(piece, "core", [(0, 1), (1, 0)]) for piece in mine]

    places = buffers(lengths, store=(micros, rows, width), masked=(members, micros, rows, width // members))
    store, masked = places["store"], places["masked"]
    base = upper_product(lengths, weight, cot, 0)
    state = dict(inputs=inputs, cot=cot, base=base, gain=norm_gain, **first)
    gain_acc = jnp.zeros((1, hidden), jnp.float32)

    steps = SKEW * (sections - 1) + micros
    arriving = {}
    uppers = []
    for step in range(steps):
        incoming = arriving.get(step)
        last = step == steps - 1
        depth = min(step // SKEW, sections - 1)
        while len(uppers) < depth:
            uppers.append(upper_product(lengths, weight, xups[len(uppers)], len(uppers) + 1))
        if last:
            masked = receive_step(step, lengths, cot, incoming, xups, masked)
            columns = lax.all_to_all(masked.reshape(members, micros * rows, width // members), RING, 0, 0, tiled=True)
        done = layer_step(
            step, lengths, weight, not last, state, incoming, xups[:depth], uppers,
            gain_acc, store, None if last else masked, last,
        )
        gain_acc, store = done["gout"], done["store"]
        if last:
            break
        masked = done["masked"]
        route = [
            (src, src - 1)
            for src in range(1, sections)
            if 0 <= step - SKEW * (sections - 1 - src) < micros
        ]
        if route:
            arriving[step + SKEW] = lax.ppermute(done["message"], "section", route)

    packed = product(lengths, mine, theirs, columns, gain_acc, replicas)
    block = lax.all_to_all(packed, PLANE, 0, 0, tiled=True)
    proj, gain = unpack(block, hidden // replicas, width)
    return (store[None, None], proj[None], gain)


def solution(mesh):
    sections, plane = mesh.devices.shape
    core = 2
    side = math.isqrt(plane // core)
    fine = Mesh(mesh.devices.reshape(sections, side, side, core), ("section", *PLANE))
    placed = (
        P("section", PLANE, None, None, None),
        P(PLANE, None, None, None),
        P("section", None, None),
        P("section", None),
        P(PLANE, None),
    )
    return jax.shard_map(
        per_device,
        mesh=fine,
        in_specs=placed,
        out_specs=(
            P("section", PLANE, None, None, None),
            P("section", PLANE, None),
            P("section", PLANE),
        ),
        check_vma=False,
    )
```

```python
import math
from types import SimpleNamespace

import jax
import jax.numpy as jnp
from jax import lax
from jax.experimental import pallas as pl
from jax.experimental.pallas import tpu as pltpu
from jax.sharding import Mesh
from jax.sharding import PartitionSpec as P

HEAD = 128
NORM_EPS = 1e-06
SCORE_FACTOR = 0.6
MASKED_SCORE = -1e30
RING = ("x", "core")
PLANE = ("x", "y", "core")
SKEW = 2
CHUNK = 256
LIMIT = 56 << 20
TIGHT = 10 << 20
GROUP = 16
WINDOW = 2
PARTS = 3
EXTRA = 16


VMEM = pl.BlockSpec(memory_space=pltpu.VMEM)
SMEM = pl.BlockSpec(memory_space=pltpu.SMEM)
FAR = pl.BlockSpec(memory_space=pltpu.HBM)


def dot_nt(a, b):
    return lax.dot_general(a, b, (((1,), (1,)), ((), ())), preferred_element_type=jnp.float32)


def dot_nn(a, b):
    return lax.dot_general(a, b, (((1,), (0,)), ((), ())), preferred_element_type=jnp.float32)


def dot_tn(a, b):
    return lax.dot_general(a, b, (((0,), (0,)), ((), ())), preferred_element_type=jnp.float32)


def kernel(name, body, operands, outs, scratch, sems, aliases=(), near=(), flops=0, moved=0, limit=LIMIT):
    sizes = {key: len(value) for key, value in (*operands.items(), *scratch.items()) if isinstance(value, list)}

    def flat(items):
        return [one for value in items.values() for one in (value if isinstance(value, list) else [value])]

    def run(*refs):
        refs = iter(refs)
        named = {}
        for key in (*operands, *outs, *scratch):
            named[key] = [next(refs) for _ in range(sizes[key])] if key in sizes else next(refs)
        body(SimpleNamespace(**named, sems=next(refs)))

    order = {key: sum(sizes.get(k, 1) for k in list(operands)[:i]) for i, key in enumerate(operands)}
    in_specs = []
    for key in operands:
        in_specs += [SMEM if key == "lengths" else VMEM if key in near else FAR] * sizes.get(key, 1)
    values = pl.pallas_call(
        run,
        name=name,
        in_specs=in_specs,
        out_specs=[VMEM if key in near else FAR for key in outs],
        out_shape=[jax.ShapeDtypeStruct(*item) for item in outs.values()],
        scratch_shapes=[pltpu.VMEM(*item) for item in flat(scratch)] + [pltpu.SemaphoreType.DMA((sems,))],
        input_output_aliases={order[key + "_in"]: list(outs).index(key) for key in aliases},
        compiler_params=pltpu.CompilerParams(vmem_limit_bytes=limit),
        cost_estimate=pl.CostEstimate(flops=flops, bytes_accessed=moved, transcendentals=0),
    )(*flat(operands))
    return dict(zip(outs, values))


def prelude(lengths, inputs, gain):
    micros, rows, width = inputs.shape
    hidden = gain.shape[1]
    heads = hidden // HEAD
    scale = SCORE_FACTOR / math.sqrt(HEAD)

    def body(r):
        loads = [
            pltpu.make_async_copy(r.inputs.at[micro], r.x.at[micro], r.sems.at[micro]) for micro in range(micros)
        ]
        for load in loads:
            load.start()
        writes = [pltpu.make_async_copy(r.x.at[:, :, pl.ds(hidden, width - hidden)], r.upper, r.sems.at[micros])]
        for load in loads:
            load.wait()
        writes[0].start()
        pairs = [
            (r.attended_v, r.attended), (r.shared_v, r.shared), (r.probs_v, r.probs), (r.turned_v, r.turned),
            (r.inv_v, r.inv),
        ]

        def write_back(micro, action):
            for index, (source, target) in enumerate(pairs):
                sem = r.sems.at[micros + 1 + len(pairs) * micro + index]
                action(pltpu.make_async_copy(source.at[micro], target.at[micro], sem))

        @pl.loop(0, micros)
        def _(micro):
            x = r.x[micro].astype(jnp.float32)
            inv = lax.rsqrt(jnp.mean(x * x, axis=1, keepdims=True) + NORM_EPS)
            r.inv_v[micro] = jnp.broadcast_to(inv, (rows, HEAD))
            r.shared_v[micro] = (x[:, :hidden] * inv * r.gain[...]).astype(jnp.bfloat16)
            live = lax.broadcasted_iota(jnp.int32, (rows, rows), 1) < r.lengths[0, micro]
            for head in range(heads):
                cols = slice(head * HEAD, (head + 1) * HEAD)
                shared = r.shared_v[micro, :, cols]
                scores = jnp.where(live, dot_nt(shared, shared) * scale, MASKED_SCORE)
                exponent = jnp.exp(scores - jnp.max(scores, axis=1, keepdims=True))
                probs = exponent / jnp.sum(exponent, axis=1, keepdims=True)
                r.probs_v[micro, head] = probs
                r.turned_v[micro, head] = probs.T.astype(jnp.bfloat16)
                r.attended_v[micro, :, cols] = dot_nn(probs.astype(jnp.bfloat16), shared).astype(jnp.bfloat16)
            write_back(micro, lambda made: made.start())

        @pl.loop(0, micros)
        def _(micro):
            write_back(micro, lambda made: made.wait())

        writes[0].wait()

    wide = ((micros, rows, hidden), jnp.bfloat16)
    square = (micros, heads, rows, rows)
    outs = dict(
        attended=wide, shared=wide, probs=(square, jnp.float32), turned=(square, jnp.bfloat16),
        inv=((micros, rows, HEAD), jnp.float32), upper=((micros, rows, width - hidden), jnp.bfloat16),
    )
    scratch = dict(
        x=(inputs.shape, jnp.bfloat16), attended_v=wide, shared_v=wide, probs_v=outs["probs"],
        turned_v=outs["turned"], inv_v=outs["inv"],
    )
    return kernel(
        "prelude", body, dict(lengths=lengths, inputs=inputs, gain=gain), outs, scratch,
        6 * micros + 1, near=("gain",), flops=12_000_000_000, moved=8_000_000, limit=TIGHT,
    )


def place(step, micros):
    above = lax.axis_size("section") - 1 - lax.axis_index("section")
    micro = step - SKEW * above
    active = jnp.logical_and(micro >= 0, micro < micros)
    return active, jnp.clip(micro, 0, micros - 1), above


def turned_dot(weight, rows_from, micros):
    turned = dot_nt(weight, rows_from).T
    return turned.reshape(micros, turned.shape[0] // micros, turned.shape[1])


def upper_product(lengths, kept, given, least):
    hidden, width = kept.shape
    micros, rows, wide = given.shape
    upper = width - hidden
    chunks = hidden // CHUNK

    def body(r):
        above = lax.axis_size("section") - 1 - lax.axis_index("section")

        @pl.when(above >= least)
        def _():
            load = pltpu.make_async_copy(r.given.at[:, :, pl.ds(wide - upper, upper)], r.given_v, r.sems.at[0])
            load.start()
            load.wait()
            given = r.given_v[...].reshape(micros * rows, upper)

            @pl.loop(0, chunks)
            def _(index):
                part = pl.ds(pl.multiple_of(index * CHUNK, CHUNK), CHUNK)
                r.total[:, :, part] = turned_dot(r.kept[part, hidden:], given, micros)

            write = pltpu.make_async_copy(r.total, r.out, r.sems.at[1])
            write.start()
            write.wait()

    shape = ((micros, rows, hidden), jnp.float32)
    return kernel(
        "upper_product", body, dict(lengths=lengths, kept=kept, given=given), dict(out=shape),
        dict(given_v=((micros, rows, upper), jnp.bfloat16), total=shape),
        2, near=("kept",), flops=200_000_000, moved=300_000, limit=TIGHT,
    )["out"]


def coefficients(message, hidden, count):
    found = []
    for far in range(count):
        coef = jnp.zeros((message.shape[0], 1), jnp.float32)
        for part in reversed(range(PARTS)):
            at = hidden + far * PARTS + part
            coef = coef + message[:, at : at + 1].astype(jnp.float32)
        found.append(coef)
    return found


def rebuild(above, raw, ups, coefs, hidden):
    high = raw[:, hidden:]
    for far in reversed(range(len(coefs))):
        value = (high.astype(jnp.float32) - ups[far][...].astype(jnp.float32) * coefs[far]).astype(jnp.bfloat16)
        high = jnp.where(above > far, value, high)
    raw[:, hidden:] = high


def cut(length, raw, tiles):
    rows, width = raw.shape
    keep = lax.broadcasted_iota(jnp.int32, (rows, HEAD), 0) < length
    wide = tiles.shape[2]
    for tile in range(width // HEAD):
        value = raw[:, tile * HEAD : (tile + 1) * HEAD].astype(jnp.float32)
        index, at = divmod(tile * HEAD, wide)
        tiles[index, :, at : at + HEAD] = jnp.where(keep, value, 0.0).astype(jnp.bfloat16)


def layer_step(step, lengths, weight, resident, state, incoming, xups, uppers, gain_acc, store, masked, last):
    micros, rows, width = state["inputs"].shape
    hidden = weight.shape[0]
    heads = hidden // HEAD
    chunks = hidden // CHUNK
    count = len(xups)
    scale = SCORE_FACTOR / math.sqrt(HEAD)

    operands = dict(
        lengths=lengths, weight=weight, **state, gacc=gain_acc, store_in=store, xups=list(xups), uppers=list(uppers)
    )
    aliases = ["store"]
    outs = dict(gout=((1, hidden), jnp.float32), store=(store.shape, store.dtype))
    near = ["gain", "gacc", "gout", "inc", "message"]
    if resident:
        near += ["weight", *state, "xups", "uppers"]
    half = ((rows, hidden), jnp.bfloat16)
    half_float = ((rows, hidden), jnp.float32)
    full = ((rows, width), jnp.bfloat16)
    scratch = dict(raw=full, sums=half_float, scaled=half_float, grad=full, inner=((rows, HEAD), jnp.float32))
    if not resident:
        scratch |= dict(
            block=((chunks, CHUNK, hidden), jnp.bfloat16), base_v=half_float, shared_v=half,
            probs_v=((heads, rows, rows), jnp.float32), turned_v=((heads, rows, rows), jnp.bfloat16),
            inv_v=((rows, HEAD), jnp.float32), x_v=full, cot_v=full, ups_v=[half] * count,
            uppers_v=[half_float] * count,
        )
    if masked is not None:
        operands["masked_in"] = masked
        outs["masked"] = (masked.shape, masked.dtype)
        scratch["tiles"] = ((masked.shape[0], rows, masked.shape[3]), jnp.bfloat16)
        aliases.append("masked")
    if incoming is not None:
        operands["inc"] = incoming
    if not last:
        outs["message"] = ((rows, hidden + HEAD), jnp.bfloat16)

    def body(r):
        active, micro, above = place(step, micros)
        used = []

        def copy(source, target):
            made = pltpu.make_async_copy(source, target, r.sems.at[len(used)])
            used.append(made)
            return made

        def guarded(far, action):
            @pl.when(above > far)
            def _():
                action()

        @pl.when(jnp.logical_not(active))
        def _():
            r.gout[...] = r.gacc[...]

        @pl.when(active)
        def _():
            if resident:
                cot, base, probs_of, shared_of, turned_of, inv_of, x = (
                    ref.at[micro] for ref in (r.cot, r.base, r.probs, r.shared, r.turned, r.inv, r.inputs)
                )
                ups = [ref.at[micro] for ref in r.xups]
                products = [ref.at[micro] for ref in r.uppers]
            else:
                cot, base, probs_of, shared_of, turned_of, inv_of, x = (
                    r.cot_v, r.base_v, r.probs_v, r.shared_v, r.turned_v, r.inv_v, r.x_v
                )
                ups, products = r.ups_v, r.uppers_v
                sources = (r.cot, r.base, r.probs, r.shared, r.turned, r.inv, r.inputs)
                targets = (cot, base, probs_of, shared_of, turned_of, inv_of, x)
                loads = [copy(source.at[micro], target) for source, target in zip(sources, targets)]
                loads[0].start()
                blocks = []
                for index in range(chunks):
                    source = r.weight.at[pl.ds(index * CHUNK, CHUNK), pl.ds(0, hidden)]
                    blocks.append(copy(source, r.block.at[index]))
                for block in blocks[:WINDOW]:
                    block.start()
                far_loads = [copy(r.uppers[far].at[micro], products[far]) for far in range(count)]
                far_loads += [copy(r.xups[far].at[micro], ups[far]) for far in range(count)]
                loads[0].wait()

            length = r.lengths[0, micro]
            coefs = []
            r.raw[:, :hidden] = cot[:, :hidden]
            if incoming is not None:
                @pl.when(above > 0)
                def _():
                    r.raw[:, :hidden] = r.inc[:, :hidden]

                coefs = coefficients(r.inc[...], hidden, count)
            if resident:
                turns = chunks // 2
                wide = 2 * CHUNK
                keep_wide = lax.broadcasted_iota(jnp.int32, (rows, wide), 0) < length

                @pl.loop(0, turns)
                def _(turn):
                    for side in range(2):
                        part = pl.ds(pl.multiple_of(turn * wide + side * CHUNK, CHUNK), CHUNK)
                        r.sums[:, part] = dot_nt(r.weight[part, :hidden], r.raw[:, :hidden]).T
                    low_part = pl.ds(pl.multiple_of(turn * wide, wide), wide)
                    high_part = pl.ds(pl.multiple_of(hidden + turn * wide, wide), wide)
                    high = cot[:, high_part]
                    for far in reversed(range(count)):
                        value = high.astype(jnp.float32) - ups[far][:, low_part].astype(jnp.float32) * coefs[far]
                        high = jnp.where(above > far, value.astype(jnp.bfloat16), high)
                    r.raw[:, high_part] = high
                    for index, value in ((turn, r.raw[:, low_part]), (turns + turn, high)):
                        r.tiles[index] = jnp.where(keep_wide, value.astype(jnp.float32), 0.0).astype(jnp.bfloat16)

                tile_copy = copy(r.tiles, r.masked.at[:, micro])
                tile_copy.start()
            else:
                r.raw[:, hidden:] = cot[:, hidden:]
                for index in range(chunks):
                    blocks[index].wait()
                    if index + WINDOW < chunks:
                        blocks[index + WINDOW].start()
                    elif index + WINDOW == chunks:
                        for made in loads[1:]:
                            made.start()
                        for index_far, made in enumerate(far_loads):
                            guarded(index_far % count, made.start)
                    r.sums[:, index * CHUNK : (index + 1) * CHUNK] = dot_nt(r.block[index], r.raw[:, :hidden]).T
                for made in loads[1:]:
                    made.wait()
                for index_far, made in enumerate(far_loads):
                    guarded(index_far % count, made.wait)
                rebuild(above, r.raw, ups, coefs, hidden)
            r.sums[...] += base[...]
            for far in range(count):
                @pl.when(above > far)
                def _():
                    r.sums[...] -= coefs[far] * products[far][...]

            keep = lax.broadcasted_iota(jnp.int32, (rows, HEAD), 0) < length
            inv = inv_of[...]
            r.inner[...] = jnp.zeros((rows, HEAD), jnp.float32)

            @pl.loop(0, heads // GROUP)
            def _(group):
                inner = r.inner[...]
                for local in range(GROUP):
                    head = group * GROUP + local
                    cols = pl.ds(pl.multiple_of(head * HEAD, HEAD), HEAD)
                    shared = shared_of[:, cols]
                    probs = probs_of[head]
                    grad_head = jnp.where(keep, r.sums[:, cols], 0.0).astype(jnp.bfloat16)
                    grad_probs = dot_nt(grad_head, shared)
                    delta = jnp.sum(probs * grad_probs, axis=1, keepdims=True)
                    dscore = scale * probs * (grad_probs - delta)
                    left = jnp.concatenate([(dscore + dscore.T).astype(jnp.bfloat16), turned_of[head]], axis=1)
                    grad_shared = dot_nn(left, jnp.concatenate([shared, grad_head], axis=0))
                    x_head = x[:, cols].astype(jnp.float32)
                    gain_term = jnp.sum(grad_shared * (x_head * inv), axis=0, keepdims=True)
                    r.gout[:, cols] = r.gacc[:, cols] + gain_term
                    scaled = grad_shared * r.gain[:, cols]
                    inner = inner + scaled * x_head
                    r.scaled[:, cols] = scaled
                r.inner[...] = inner

            inner = r.inner[...]
            inv = inv[:, :1]
            coef = inv * inv * inv * (jnp.sum(inner, axis=1, keepdims=True) / width)
            low = r.raw[:, :hidden].astype(jnp.float32) + inv * r.scaled[...]
            low = (low - x[:, :hidden].astype(jnp.float32) * coef).astype(jnp.bfloat16)
            r.grad[:, :hidden] = low
            if not last:
                r.message[:, :hidden] = low
                lane = lax.broadcasted_iota(jnp.int32, (rows, HEAD), 1)
                if incoming is None:
                    tail = jnp.zeros((rows, HEAD), jnp.float32)
                else:
                    came = jnp.where(above == 0, 0.0, r.inc[:, hidden:].astype(jnp.float32))
                    tail = jnp.where(lane < PARTS, 0.0, pltpu.roll(came, PARTS, axis=1))
                left_over = coef
                for part in range(PARTS):
                    piece = left_over.astype(jnp.bfloat16).astype(jnp.float32)
                    tail = jnp.where(lane == part, piece, tail)
                    left_over = left_over - piece
                r.message[:, hidden:] = tail.astype(jnp.bfloat16)
            high = r.raw[:, hidden:].astype(jnp.float32) - x[:, hidden:].astype(jnp.float32) * coef
            r.grad[:, hidden:] = high.astype(jnp.bfloat16)
            keeper = copy(r.grad, r.store.at[micro])
            keeper.start()
            if resident:
                tile_copy.wait()
            keeper.wait()

    return kernel(
        "layer_step", body, operands, outs, scratch, chunks + 2 * count + 12, aliases,
        near=near, flops=500_000_000, moved=1_000_000, limit=TIGHT if resident else LIMIT,
    )


def receive_step(step, lengths, cot, incoming, xups, masked):
    micros, rows, width = cot.shape
    hidden = incoming.shape[1] - HEAD
    count = len(xups)

    def body(r):
        active, micro, above = place(step, micros)

        @pl.when(active)
        def _():
            loads = [pltpu.make_async_copy(r.cot.at[micro], r.raw, r.sems.at[1])]
            for far in range(count):
                loads.append(pltpu.make_async_copy(r.xups[far].at[micro], r.ups_v[far], r.sems.at[2 + far]))
            for load in loads:
                load.start()
            for load in loads:
                load.wait()

            @pl.when(above > 0)
            def _():
                r.raw[:, :hidden] = r.inc[:, :hidden]

            rebuild(above, r.raw, r.ups_v, coefficients(r.inc[...], hidden, count), hidden)
            cut(r.lengths[0, micro], r.raw, r.tiles)
            write = pltpu.make_async_copy(r.tiles, r.masked.at[:, micro], r.sems.at[0])
            write.start()
            write.wait()

    return kernel(
        "receive_step", body, dict(lengths=lengths, cot=cot, inc=incoming, masked_in=masked, xups=list(xups)),
        dict(masked=(masked.shape, masked.dtype)),
        dict(
            raw=((rows, width), jnp.bfloat16), tiles=((masked.shape[0], rows, masked.shape[3]), jnp.bfloat16),
            ups_v=[((rows, width - hidden), jnp.bfloat16)] * count,
        ),
        2 + count, ["masked"], near=("inc",), flops=1_000_000, moved=2_000_000, limit=TIGHT,
    )["masked"]


def buffers(lengths, **shapes):
    outs = {key: (shape, jnp.bfloat16) for key, shape in shapes.items()}
    return kernel("buffers", lambda r: None, dict(lengths=lengths), outs, {}, 1, limit=1 << 20)


def product(lengths, mine, theirs, columns, gain, owners):
    depth, hidden = mine[0].shape
    members, _, wide = columns.shape
    own = hidden // owners
    turns = members // 2
    rows = own * wide // HEAD + EXTRA

    def body(r):
        place_x = lax.axis_index("x")
        core = lax.axis_index("core")
        loads = []
        for turn in range(turns):
            behind = lax.rem(place_x - turn + turns, turns)
            for side, pieces in enumerate((r.mine, r.theirs)):
                member = behind * 2 + (core if side == 0 else 1 - core)
                made = pltpu.make_async_copy(pieces[turn], r.stack.at[member], r.sems.at[2 * turn + side])
                made.start()
                loads.append(made)
        for member in range(members):
            r.turned[:, member * depth : (member + 1) * depth] = r.columns[member].T
        for made in loads:
            made.wait()
        span = 2 * CHUNK
        for start in range(0, hidden, span):
            right = r.stack[:, :, start : start + span].reshape(members * depth, span)
            sums = dot_nn(r.turned[...], right)
            for owner in range(start // own, (start + span) // own, 2):
                at = owner * own - start
                gains = jnp.broadcast_to(r.gain[:, owner * own : (owner + 2) * own], (EXTRA, HEAD))
                for tile in range(wide // HEAD):
                    block = sums[tile * HEAD : (tile + 1) * HEAD, at : at + HEAD].T.astype(jnp.bfloat16)
                    for side in range(2):
                        r.out[owner + side, tile * own : (tile + 1) * own] = block[side * own : (side + 1) * own]
                for side in range(2):
                    r.out[owner + side, rows - EXTRA :] = gains.astype(jnp.bfloat16)

    return kernel(
        "product", body,
        dict(lengths=lengths, mine=list(mine), theirs=list(theirs), columns=columns, gain=gain),
        dict(out=((owners, rows, HEAD), jnp.bfloat16)),
        dict(
            stack=((members, depth, hidden), jnp.bfloat16), turned=((wide, members * depth), jnp.bfloat16),
        ),
        members, near=("columns", "gain", "out"), flops=2 * members * depth * hidden * wide,
        moved=2 * members * depth * (hidden + wide), limit=LIMIT,
    )["out"]


def unpack(block, own, width):
    sources, rows, _ = block.shape
    wide = (rows - EXTRA) // own * HEAD

    def body(block_ref, proj_ref, gain_ref):
        rings = lax.axis_size("y")
        total = jnp.zeros((EXTRA, HEAD), jnp.float32)
        for member in range(width // wide):
            place_x, core = divmod(member, 2)
            froms = [(place_x * rings + ring) * 2 + core for ring in range(rings)]
            for tile in range(wide // HEAD):
                value = jnp.zeros((own, HEAD), jnp.float32)
                for source in froms:
                    value = value + block_ref[source, tile * own : (tile + 1) * own].astype(jnp.float32)
                at = member * wide + tile * HEAD
                proj_ref[:, at : at + HEAD] = value
            for source in froms:
                total = total + block_ref[source, rows - EXTRA :].astype(jnp.float32)
        odd = lax.axis_index("core") == 1
        gain_ref[...] = jnp.where(odd, total[:1, own:], total[:1, :own])

    return pl.pallas_call(
        body,
        name="unpack",
        in_specs=[VMEM],
        out_specs=[VMEM] * 2,
        out_shape=[
            jax.ShapeDtypeStruct((own, width), jnp.float32),
            jax.ShapeDtypeStruct((1, own), jnp.float32),
        ],
        compiler_params=pltpu.CompilerParams(vmem_limit_bytes=TIGHT),
    )(block)


def per_device(saved_inputs, cotangent, out_proj, norm_gain, lengths):
    sections = lax.axis_size("section")
    replicas = lax.axis_size(PLANE)
    members = lax.axis_size(RING)
    inputs = saved_inputs[0, 0]
    cot = cotangent[0]
    weight = out_proj[0]
    micros, rows, width = inputs.shape
    hidden = weight.shape[0]

    first = prelude(lengths, inputs, norm_gain)
    attended = first.pop("attended").reshape(micros * rows, hidden)
    own_up = first.pop("upper")
    round_once = lax.ppermute(own_up, "section", [(3, 0), (2, 3)])
    near = lax.ppermute(own_up, "section", [(3, 2), (2, 1), (1, 0)])
    turns = lax.axis_size("x")
    ahead = [(i, (i + 1) % turns) for i in range(turns)]
    back = [((i + 1) % turns, i) for i in range(turns)]
    one = lax.ppermute(attended, "x", ahead)
    three = lax.ppermute(attended, "x", back)
    two = lax.ppermute(one, "x", ahead)
    mine = [attended, one, two, three]
    theirs = [lax.ppermute(piece, "core", [(0, 1), (1, 0)]) for piece in mine]

    places = buffers(lengths, store=(micros, rows, width), masked=(members, micros, rows, width // members))
    store, masked = places["store"], places["masked"]
    base = upper_product(lengths, weight, cot, 0)
    state = dict(inputs=inputs, cot=cot, base=base, gain=norm_gain, **first)
    gain_acc = jnp.zeros((1, hidden), jnp.float32)

    steps = SKEW * (sections - 1) + micros
    arriving = {}
    uppers = []
    xups = []
    for step in range(steps):
        if step == 1:
            round_once, gain_acc = lax.optimization_barrier((round_once, gain_acc))
            round_twice = lax.ppermute(round_once, "section", [(0, 1), (3, 0)])
            xups = [near, round_twice, round_once]
        incoming = arriving.get(step)
        last = step == steps - 1
        depth = min(step // SKEW, sections - 1)
        while len(uppers) < depth:
            uppers.append(upper_product(lengths, weight, xups[len(uppers)], len(uppers) + 1))
        if last:
            masked = receive_step(step, lengths, cot, incoming, xups, masked)
            columns = lax.all_to_all(masked.reshape(members, micros * rows, width // members), RING, 0, 0, tiled=True)
        done = layer_step(
            step, lengths, weight, not last, state, incoming, xups[:depth] if depth else [], uppers,
            gain_acc, store, None if last else masked, last,
        )
        gain_acc, store = done["gout"], done["store"]
        if last:
            break
        masked = done["masked"]
        route = [
            (src, src - 1)
            for src in range(1, sections)
            if 0 <= step - SKEW * (sections - 1 - src) < micros
        ]
        if route:
            arriving[step + SKEW] = lax.ppermute(done["message"], "section", route)

    packed = product(lengths, mine, theirs, columns, gain_acc, replicas)
    block = lax.all_to_all(packed, PLANE, 0, 0, tiled=True)
    proj, gain = unpack(block, hidden // replicas, width)
    return (store[None, None], proj[None], gain)


def solution(mesh):
    sections, plane = mesh.devices.shape
    core = 2
    side = math.isqrt(plane // core)
    fine = Mesh(mesh.devices.reshape(sections, side, side, core), ("section", *PLANE))
    placed = (
        P("section", PLANE, None, None, None),
        P(PLANE, None, None, None),
        P("section", None, None),
        P("section", None),
        P(PLANE, None),
    )
    return jax.shard_map(
        per_device,
        mesh=fine,
        in_specs=placed,
        out_specs=(
            P("section", PLANE, None, None, None),
            P("section", PLANE, None),
            P("section", PLANE),
        ),
        check_vma=False,
    )
```

```python
import math
from types import SimpleNamespace

import jax
import jax.numpy as jnp
from jax import lax
from jax.experimental import pallas as pl
from jax.experimental.pallas import tpu as pltpu
from jax.sharding import Mesh
from jax.sharding import PartitionSpec as P

HEAD = 128
NORM_EPS = 1e-06
SCORE_FACTOR = 0.6
MASKED_SCORE = -1e30
RING = ("x", "core")
PLANE = ("x", "y", "core")
SKEW = 2
CHUNK = 256
LIMIT = 56 << 20
TIGHT = 10 << 20
GROUP = 16
WINDOW = 2
PARTS = 3
EXTRA = 16


VMEM = pl.BlockSpec(memory_space=pltpu.VMEM)
SMEM = pl.BlockSpec(memory_space=pltpu.SMEM)
FAR = pl.BlockSpec(memory_space=pltpu.HBM)


def dot_nt(a, b):
    return lax.dot_general(a, b, (((1,), (1,)), ((), ())), preferred_element_type=jnp.float32)


def dot_nn(a, b):
    return lax.dot_general(a, b, (((1,), (0,)), ((), ())), preferred_element_type=jnp.float32)


def dot_tn(a, b):
    return lax.dot_general(a, b, (((0,), (0,)), ((), ())), preferred_element_type=jnp.float32)


def kernel(name, body, operands, outs, scratch, sems, aliases=(), near=(), flops=0, moved=0, limit=LIMIT):
    sizes = {key: len(value) for key, value in (*operands.items(), *scratch.items()) if isinstance(value, list)}

    def flat(items):
        return [one for value in items.values() for one in (value if isinstance(value, list) else [value])]

    def run(*refs):
        refs = iter(refs)
        named = {}
        for key in (*operands, *outs, *scratch):
            named[key] = [next(refs) for _ in range(sizes[key])] if key in sizes else next(refs)
        body(SimpleNamespace(**named, sems=next(refs)))

    order = {key: sum(sizes.get(k, 1) for k in list(operands)[:i]) for i, key in enumerate(operands)}
    in_specs = []
    for key in operands:
        in_specs += [SMEM if key == "lengths" else VMEM if key in near else FAR] * sizes.get(key, 1)
    values = pl.pallas_call(
        run,
        name=name,
        in_specs=in_specs,
        out_specs=[VMEM if key in near else FAR for key in outs],
        out_shape=[jax.ShapeDtypeStruct(*item) for item in outs.values()],
        scratch_shapes=[pltpu.VMEM(*item) for item in flat(scratch)] + [pltpu.SemaphoreType.DMA((sems,))],
        input_output_aliases={order[key + "_in"]: list(outs).index(key) for key in aliases},
        compiler_params=pltpu.CompilerParams(vmem_limit_bytes=limit),
        cost_estimate=pl.CostEstimate(flops=flops, bytes_accessed=moved, transcendentals=0),
    )(*flat(operands))
    return dict(zip(outs, values))


def prelude(lengths, inputs, gain):
    micros, rows, width = inputs.shape
    hidden = gain.shape[1]
    heads = hidden // HEAD
    scale = SCORE_FACTOR / math.sqrt(HEAD)

    def body(r):
        loads = [
            pltpu.make_async_copy(r.inputs.at[micro], r.x.at[micro], r.sems.at[micro]) for micro in range(micros)
        ]
        for load in loads:
            load.start()
        for load in loads:
            load.wait()
        pairs = [
            (r.attended_v, r.attended), (r.shared_v, r.shared), (r.probs_v, r.probs), (r.turned_v, r.turned),
            (r.inv_v, r.inv),
        ]

        def write_back(micro, action):
            for index, (source, target) in enumerate(pairs):
                sem = r.sems.at[micros + len(pairs) * micro + index]
                action(pltpu.make_async_copy(source.at[micro], target.at[micro], sem))

        @pl.loop(0, micros, unroll=True)
        def _(micro):
            x = r.x[micro].astype(jnp.float32)
            inv = lax.rsqrt(jnp.mean(x * x, axis=1, keepdims=True) + NORM_EPS)
            r.inv_v[micro] = jnp.broadcast_to(inv, (rows, HEAD))
            r.shared_v[micro] = (x[:, :hidden] * inv * r.gain[...]).astype(jnp.bfloat16)
            live = lax.broadcasted_iota(jnp.int32, (rows, rows), 1) < r.lengths[0, micro]
            for head in range(heads):
                cols = slice(head * HEAD, (head + 1) * HEAD)
                shared = r.shared_v[micro, :, cols]
                scores = jnp.where(live, dot_nt(shared, shared) * scale, MASKED_SCORE)
                exponent = jnp.exp(scores - jnp.max(scores, axis=1, keepdims=True))
                probs = exponent / jnp.sum(exponent, axis=1, keepdims=True)
                r.probs_v[micro, head] = probs
                r.turned_v[micro, head] = probs.T.astype(jnp.bfloat16)
                r.attended_v[micro, :, cols] = dot_nn(probs.astype(jnp.bfloat16), shared).astype(jnp.bfloat16)
            write_back(micro, lambda made: made.start())

        @pl.loop(0, micros)
        def _(micro):
            write_back(micro, lambda made: made.wait())

    wide = ((micros, rows, hidden), jnp.bfloat16)
    square = (micros, heads, rows, rows)
    outs = dict(
        attended=wide, shared=wide, probs=(square, jnp.float32), turned=(square, jnp.bfloat16),
        inv=((micros, rows, HEAD), jnp.float32),
    )
    scratch = dict(
        x=(inputs.shape, jnp.bfloat16), attended_v=wide, shared_v=wide, probs_v=outs["probs"],
        turned_v=outs["turned"], inv_v=outs["inv"],
    )
    return kernel(
        "prelude", body, dict(lengths=lengths, inputs=inputs, gain=gain), outs, scratch,
        6 * micros, near=("gain",), flops=12_000_000_000, moved=8_000_000, limit=TIGHT,
    )


def lift(lengths, inputs, hidden):
    micros, rows, width = inputs.shape

    def body(r):
        made = pltpu.make_async_copy(r.inputs.at[:, :, pl.ds(hidden, width - hidden)], r.out, r.sems.at[0])
        made.start()
        made.wait()

    outs = dict(out=((micros, rows, width - hidden), jnp.bfloat16))
    return kernel("lift", body, dict(lengths=lengths, inputs=inputs), outs, {}, 1, limit=TIGHT)["out"]


def place(step, micros):
    above = lax.axis_size("section") - 1 - lax.axis_index("section")
    micro = step - SKEW * above
    active = jnp.logical_and(micro >= 0, micro < micros)
    return active, jnp.clip(micro, 0, micros - 1), above


def turned_dot(weight, rows_from, micros):
    turned = dot_nt(weight, rows_from).T
    return turned.reshape(micros, turned.shape[0] // micros, turned.shape[1])


def upper_product(lengths, kept, given, least):
    hidden, width = kept.shape
    micros, rows, wide = given.shape
    upper = width - hidden
    chunks = hidden // CHUNK

    def body(r):
        above = lax.axis_size("section") - 1 - lax.axis_index("section")

        @pl.when(above >= least)
        def _():
            load = pltpu.make_async_copy(r.given.at[:, :, pl.ds(wide - upper, upper)], r.given_v, r.sems.at[0])
            load.start()
            load.wait()
            given = r.given_v[...].reshape(micros * rows, upper)

            @pl.loop(0, chunks, unroll=4)
            def _(index):
                part = pl.ds(pl.multiple_of(index * CHUNK, CHUNK), CHUNK)
                r.total[:, :, part] = turned_dot(r.kept[part, hidden:], given, micros)

            write = pltpu.make_async_copy(r.total, r.out, r.sems.at[1])
            write.start()
            write.wait()

    shape = ((micros, rows, hidden), jnp.float32)
    return kernel(
        "upper_product", body, dict(lengths=lengths, kept=kept, given=given), dict(out=shape),
        dict(given_v=((micros, rows, upper), jnp.bfloat16), total=shape),
        2, near=("kept",), flops=200_000_000, moved=300_000, limit=TIGHT,
    )["out"]


def coefficients(message, hidden, count):
    found = []
    for far in range(count):
        coef = jnp.zeros((message.shape[0], 1), jnp.float32)
        for part in reversed(range(PARTS)):
            at = hidden + far * PARTS + part
            coef = coef + message[:, at : at + 1].astype(jnp.float32)
        found.append(coef)
    return found


def rebuild(above, raw, ups, coefs, hidden):
    high = raw[:, hidden:]
    for far in reversed(range(len(coefs))):
        value = (high.astype(jnp.float32) - ups[far][...].astype(jnp.float32) * coefs[far]).astype(jnp.bfloat16)
        high = jnp.where(above > far, value, high)
    raw[:, hidden:] = high


def cut(length, raw, tiles):
    rows, width = raw.shape
    keep = lax.broadcasted_iota(jnp.int32, (rows, HEAD), 0) < length
    wide = tiles.shape[2]
    for tile in range(width // HEAD):
        value = raw[:, tile * HEAD : (tile + 1) * HEAD].astype(jnp.float32)
        index, at = divmod(tile * HEAD, wide)
        tiles[index, :, at : at + HEAD] = jnp.where(keep, value, 0.0).astype(jnp.bfloat16)


def layer_step(step, lengths, weight, resident, state, incoming, xups, uppers, gain_acc, store, masked, last):
    micros, rows, width = state["inputs"].shape
    hidden = weight.shape[0]
    heads = hidden // HEAD
    chunks = hidden // CHUNK
    count = len(xups)
    scale = SCORE_FACTOR / math.sqrt(HEAD)

    operands = dict(
        lengths=lengths, weight=weight, **state, gacc=gain_acc, store_in=store, xups=list(xups), uppers=list(uppers)
    )
    aliases = ["store"]
    outs = dict(gout=((1, hidden), jnp.float32), store=(store.shape, store.dtype))
    near = ["gain", "gacc", "gout", "inc", "message"]
    if resident:
        near += ["weight", *state, "xups", "uppers"]
    half = ((rows, hidden), jnp.bfloat16)
    half_float = ((rows, hidden), jnp.float32)
    full = ((rows, width), jnp.bfloat16)
    scratch = dict(raw=full, sums=half_float, scaled=half_float, grad=full, inner=((rows, HEAD), jnp.float32))
    if not resident:
        scratch |= dict(
            block=((chunks, CHUNK, hidden), jnp.bfloat16), base_v=half_float, shared_v=half,
            probs_v=((heads, rows, rows), jnp.float32), turned_v=((heads, rows, rows), jnp.bfloat16),
            inv_v=((rows, HEAD), jnp.float32), x_v=full, cot_v=full, ups_v=[half] * count,
            uppers_v=[half_float] * count,
        )
    if masked is not None:
        operands["masked_in"] = masked
        outs["masked"] = (masked.shape, masked.dtype)
        scratch["tiles"] = ((masked.shape[0], rows, masked.shape[3]), jnp.bfloat16)
        aliases.append("masked")
    if incoming is not None:
        operands["inc"] = incoming
    if not last:
        outs["message"] = ((rows, hidden + HEAD), jnp.bfloat16)

    def body(r):
        active, micro, above = place(step, micros)
        used = []

        def copy(source, target):
            made = pltpu.make_async_copy(source, target, r.sems.at[len(used)])
            used.append(made)
            return made

        def guarded(far, action):
            @pl.when(above > far)
            def _():
                action()

        @pl.when(jnp.logical_not(active))
        def _():
            r.gout[...] = r.gacc[...]

        @pl.when(active)
        def _():
            if resident:
                cot, base, probs_of, shared_of, turned_of, inv_of, x = (
                    ref.at[micro] for ref in (r.cot, r.base, r.probs, r.shared, r.turned, r.inv, r.inputs)
                )
                ups = [ref.at[micro] for ref in r.xups]
                products = [ref.at[micro] for ref in r.uppers]
            else:
                cot, base, probs_of, shared_of, turned_of, inv_of, x = (
                    r.cot_v, r.base_v, r.probs_v, r.shared_v, r.turned_v, r.inv_v, r.x_v
                )
                ups, products = r.ups_v, r.uppers_v
                sources = (r.cot, r.base, r.probs, r.shared, r.turned, r.inv, r.inputs)
                targets = (cot, base, probs_of, shared_of, turned_of, inv_of, x)
                loads = [copy(source.at[micro], target) for source, target in zip(sources, targets)]
                loads[0].start()
                blocks = []
                for index in range(chunks):
                    source = r.weight.at[pl.ds(index * CHUNK, CHUNK), pl.ds(0, hidden)]
                    blocks.append(copy(source, r.block.at[index]))
                for block in blocks[:WINDOW]:
                    block.start()
                far_loads = [copy(r.uppers[far].at[micro], products[far]) for far in range(count)]
                far_loads += [copy(r.xups[far].at[micro], ups[far]) for far in range(count)]
                loads[0].wait()

            length = r.lengths[0, micro]
            coefs = []
            r.raw[:, :hidden] = cot[:, :hidden]
            if incoming is not None:
                @pl.when(above > 0)
                def _():
                    r.raw[:, :hidden] = r.inc[:, :hidden]

                coefs = coefficients(r.inc[...], hidden, count)
            if resident:
                turns = chunks // 2
                wide = 2 * CHUNK
                keep_wide = lax.broadcasted_iota(jnp.int32, (rows, wide), 0) < length

                @pl.loop(0, turns)
                def _(turn):
                    for side in range(2):
                        part = pl.ds(pl.multiple_of(turn * wide + side * CHUNK, CHUNK), CHUNK)
                        r.sums[:, part] = dot_nt(r.weight[part, :hidden], r.raw[:, :hidden]).T
                    low_part = pl.ds(pl.multiple_of(turn * wide, wide), wide)
                    high_part = pl.ds(pl.multiple_of(hidden + turn * wide, wide), wide)
                    high = cot[:, high_part]
                    for far in reversed(range(count)):
                        value = high.astype(jnp.float32) - ups[far][:, low_part].astype(jnp.float32) * coefs[far]
                        high = jnp.where(above > far, value.astype(jnp.bfloat16), high)
                    r.raw[:, high_part] = high
                    for index, value in ((turn, r.raw[:, low_part]), (turns + turn, high)):
                        r.tiles[index] = jnp.where(keep_wide, value.astype(jnp.float32), 0.0).astype(jnp.bfloat16)

                tile_copy = copy(r.tiles, r.masked.at[:, micro])
                tile_copy.start()
            else:
                r.raw[:, hidden:] = cot[:, hidden:]
                for index in range(chunks):
                    blocks[index].wait()
                    if index + WINDOW < chunks:
                        blocks[index + WINDOW].start()
                    elif index + WINDOW == chunks:
                        for made in loads[1:]:
                            made.start()
                        for index_far, made in enumerate(far_loads):
                            guarded(index_far % count, made.start)
                    r.sums[:, index * CHUNK : (index + 1) * CHUNK] = dot_nt(r.block[index], r.raw[:, :hidden]).T
                for made in loads[1:]:
                    made.wait()
                for index_far, made in enumerate(far_loads):
                    guarded(index_far % count, made.wait)
                rebuild(above, r.raw, ups, coefs, hidden)
            r.sums[...] += base[...]
            for far in range(count):
                @pl.when(above > far)
                def _():
                    r.sums[...] -= coefs[far] * products[far][...]

            keep = lax.broadcasted_iota(jnp.int32, (rows, HEAD), 0) < length
            inv = inv_of[...]
            r.inner[...] = jnp.zeros((rows, HEAD), jnp.float32)

            @pl.loop(0, heads // GROUP)
            def _(group):
                inner = r.inner[...]
                for local in range(GROUP):
                    head = group * GROUP + local
                    cols = pl.ds(pl.multiple_of(head * HEAD, HEAD), HEAD)
                    shared = shared_of[:, cols]
                    probs = probs_of[head]
                    grad_head = jnp.where(keep, r.sums[:, cols], 0.0).astype(jnp.bfloat16)
                    grad_probs = dot_nt(grad_head, shared)
                    delta = jnp.sum(probs * grad_probs, axis=1, keepdims=True)
                    dscore = scale * probs * (grad_probs - delta)
                    left = jnp.concatenate([(dscore + dscore.T).astype(jnp.bfloat16), turned_of[head]], axis=1)
                    grad_shared = dot_nn(left, jnp.concatenate([shared, grad_head], axis=0))
                    x_head = x[:, cols].astype(jnp.float32)
                    gain_term = jnp.sum(grad_shared * (x_head * inv), axis=0, keepdims=True)
                    r.gout[:, cols] = r.gacc[:, cols] + gain_term
                    scaled = grad_shared * r.gain[:, cols]
                    inner = inner + scaled * x_head
                    r.scaled[:, cols] = scaled
                r.inner[...] = inner

            inner = r.inner[...]
            inv = inv[:, :1]
            coef = inv * inv * inv * (jnp.sum(inner, axis=1, keepdims=True) / width)
            low = r.raw[:, :hidden].astype(jnp.float32) + inv * r.scaled[...]
            low = (low - x[:, :hidden].astype(jnp.float32) * coef).astype(jnp.bfloat16)
            r.grad[:, :hidden] = low
            if not last:
                r.message[:, :hidden] = low
                lane = lax.broadcasted_iota(jnp.int32, (rows, HEAD), 1)
                if incoming is None:
                    tail = jnp.zeros((rows, HEAD), jnp.float32)
                else:
                    came = jnp.where(above == 0, 0.0, r.inc[:, hidden:].astype(jnp.float32))
                    tail = jnp.where(lane < PARTS, 0.0, pltpu.roll(came, PARTS, axis=1))
                left_over = coef
                for part in range(PARTS):
                    piece = left_over.astype(jnp.bfloat16).astype(jnp.float32)
                    tail = jnp.where(lane == part, piece, tail)
                    left_over = left_over - piece
                r.message[:, hidden:] = tail.astype(jnp.bfloat16)
            high = r.raw[:, hidden:].astype(jnp.float32) - x[:, hidden:].astype(jnp.float32) * coef
            r.grad[:, hidden:] = high.astype(jnp.bfloat16)
            keeper = copy(r.grad, r.store.at[micro])
            keeper.start()
            if resident:
                tile_copy.wait()
            keeper.wait()

    return kernel(
        "layer_step", body, operands, outs, scratch, chunks + 2 * count + 12, aliases,
        near=near, flops=500_000_000, moved=1_000_000, limit=TIGHT if resident else LIMIT,
    )


def receive_step(step, lengths, cot, incoming, xups, masked):
    micros, rows, width = cot.shape
    hidden = incoming.shape[1] - HEAD
    count = len(xups)

    def body(r):
        active, micro, above = place(step, micros)

        @pl.when(active)
        def _():
            loads = [pltpu.make_async_copy(r.cot.at[micro], r.raw, r.sems.at[1])]
            for far in range(count):
                loads.append(pltpu.make_async_copy(r.xups[far].at[micro], r.ups_v[far], r.sems.at[2 + far]))
            for load in loads:
                load.start()
            for load in loads:
                load.wait()

            @pl.when(above > 0)
            def _():
                r.raw[:, :hidden] = r.inc[:, :hidden]

            rebuild(above, r.raw, r.ups_v, coefficients(r.inc[...], hidden, count), hidden)
            cut(r.lengths[0, micro], r.raw, r.tiles)
            write = pltpu.make_async_copy(r.tiles, r.masked.at[:, micro], r.sems.at[0])
            write.start()
            write.wait()

    return kernel(
        "receive_step", body, dict(lengths=lengths, cot=cot, inc=incoming, masked_in=masked, xups=list(xups)),
        dict(masked=(masked.shape, masked.dtype)),
        dict(
            raw=((rows, width), jnp.bfloat16), tiles=((masked.shape[0], rows, masked.shape[3]), jnp.bfloat16),
            ups_v=[((rows, width - hidden), jnp.bfloat16)] * count,
        ),
        2 + count, ["masked"], near=("inc",), flops=1_000_000, moved=2_000_000, limit=TIGHT,
    )["masked"]


def buffers(lengths, **shapes):
    outs = {key: (shape, jnp.bfloat16) for key, shape in shapes.items()}
    return kernel("buffers", lambda r: None, dict(lengths=lengths), outs, {}, 1, limit=1 << 20)


def product(lengths, mine, theirs, columns, gain, owners):
    depth, hidden = mine[0].shape
    members, _, wide = columns.shape
    own = hidden // owners
    turns = members // 2
    rows = own * wide // HEAD + EXTRA

    def body(r):
        place_x = lax.axis_index("x")
        core = lax.axis_index("core")
        loads = []
        for turn in range(turns):
            behind = lax.rem(place_x - turn + turns, turns)
            for side, pieces in enumerate((r.mine, r.theirs)):
                member = behind * 2 + (core if side == 0 else 1 - core)
                made = pltpu.make_async_copy(pieces[turn], r.stack.at[member], r.sems.at[2 * turn + side])
                made.start()
                loads.append(made)
        for member in range(members):
            r.turned[:, member * depth : (member + 1) * depth] = r.columns[member].T
        for made in loads:
            made.wait()
        span = 2 * CHUNK
        for start in range(0, hidden, span):
            right = r.stack[:, :, start : start + span].reshape(members * depth, span)
            sums = dot_nn(r.turned[...], right)
            for owner in range(start // own, (start + span) // own, 2):
                at = owner * own - start
                gains = jnp.broadcast_to(r.gain[:, owner * own : (owner + 2) * own], (EXTRA, HEAD))
                for tile in range(wide // HEAD):
                    block = sums[tile * HEAD : (tile + 1) * HEAD, at : at + HEAD].T.astype(jnp.bfloat16)
                    for side in range(2):
                        r.out[owner + side, tile * own : (tile + 1) * own] = block[side * own : (side + 1) * own]
                for side in range(2):
                    r.out[owner + side, rows - EXTRA :] = gains.astype(jnp.bfloat16)

    return kernel(
        "product", body,
        dict(lengths=lengths, mine=list(mine), theirs=list(theirs), columns=columns, gain=gain),
        dict(out=((owners, rows, HEAD), jnp.bfloat16)),
        dict(
            stack=((members, depth, hidden), jnp.bfloat16), turned=((wide, members * depth), jnp.bfloat16),
        ),
        members, near=("columns", "gain", "out"), flops=2 * members * depth * hidden * wide,
        moved=2 * members * depth * (hidden + wide), limit=LIMIT,
    )["out"]


def unpack(block, own, width):
    sources, rows, _ = block.shape
    wide = (rows - EXTRA) // own * HEAD

    def body(block_ref, proj_ref, gain_ref):
        rings = lax.axis_size("y")
        total = jnp.zeros((EXTRA, HEAD), jnp.float32)
        for member in range(width // wide):
            place_x, core = divmod(member, 2)
            froms = [(place_x * rings + ring) * 2 + core for ring in range(rings)]
            for tile in range(wide // HEAD):
                value = jnp.zeros((own, HEAD), jnp.float32)
                for source in froms:
                    value = value + block_ref[source, tile * own : (tile + 1) * own].astype(jnp.float32)
                at = member * wide + tile * HEAD
                proj_ref[:, at : at + HEAD] = value
            for source in froms:
                total = total + block_ref[source, rows - EXTRA :].astype(jnp.float32)
        odd = lax.axis_index("core") == 1
        gain_ref[...] = jnp.where(odd, total[:1, own:], total[:1, :own])

    return pl.pallas_call(
        body,
        name="unpack",
        in_specs=[VMEM],
        out_specs=[VMEM] * 2,
        out_shape=[
            jax.ShapeDtypeStruct((own, width), jnp.float32),
            jax.ShapeDtypeStruct((1, own), jnp.float32),
        ],
        compiler_params=pltpu.CompilerParams(vmem_limit_bytes=TIGHT),
    )(block)


def per_device(saved_inputs, cotangent, out_proj, norm_gain, lengths):
    sections = lax.axis_size("section")
    replicas = lax.axis_size(PLANE)
    members = lax.axis_size(RING)
    inputs = saved_inputs[0, 0]
    cot = cotangent[0]
    weight = out_proj[0]
    micros, rows, width = inputs.shape
    hidden = weight.shape[0]

    first = prelude(lengths, inputs, norm_gain)
    attended = first.pop("attended").reshape(micros * rows, hidden)
    own_up = lift(lengths, inputs, hidden)
    round_once = lax.ppermute(own_up, "section", [(3, 0), (2, 3)])
    near = lax.ppermute(own_up, "section", [(3, 2), (2, 1), (1, 0)])
    turns = lax.axis_size("x")
    ahead = [(i, (i + 1) % turns) for i in range(turns)]
    back = [((i + 1) % turns, i) for i in range(turns)]
    one = lax.ppermute(attended, "x", ahead)
    three = lax.ppermute(attended, "x", back)
    two = lax.ppermute(one, "x", ahead)
    mine = [attended, one, two, three]
    theirs = [lax.ppermute(piece, "core", [(0, 1), (1, 0)]) for piece in mine]

    places = buffers(lengths, store=(micros, rows, width), masked=(members, micros, rows, width // members))
    store, masked = places["store"], places["masked"]
    base = upper_product(lengths, weight, cot, 0)
    state = dict(inputs=inputs, cot=cot, base=base, gain=norm_gain, **first)
    gain_acc = jnp.zeros((1, hidden), jnp.float32)

    steps = SKEW * (sections - 1) + micros
    arriving = {}
    uppers = []
    xups = []
    for step in range(steps):
        if step == 1:
            round_once, gain_acc = lax.optimization_barrier((round_once, gain_acc))
            round_twice = lax.ppermute(round_once, "section", [(0, 1), (3, 0)])
            xups = [near, round_twice, round_once]
        incoming = arriving.get(step)
        last = step == steps - 1
        depth = min(step // SKEW, sections - 1)
        while len(uppers) < depth:
            uppers.append(upper_product(lengths, weight, xups[len(uppers)], len(uppers) + 1))
        if last:
            masked = receive_step(step, lengths, cot, incoming, xups, masked)
            columns = lax.all_to_all(masked.reshape(members, micros * rows, width // members), RING, 0, 0, tiled=True)
        done = layer_step(
            step, lengths, weight, not last, state, incoming, xups[:depth] if depth else [], uppers,
            gain_acc, store, None if last else masked, last,
        )
        gain_acc, store = done["gout"], done["store"]
        if last:
            break
        masked = done["masked"]
        route = [
            (src, src - 1)
            for src in range(1, sections)
            if 0 <= step - SKEW * (sections - 1 - src) < micros
        ]
        if route:
            arriving[step + SKEW] = lax.ppermute(done["message"], "section", route)

    packed = product(lengths, mine, theirs, columns, gain_acc, replicas)
    block = lax.all_to_all(packed, PLANE, 0, 0, tiled=True)
    proj, gain = unpack(block, hidden // replicas, width)
    return (store[None, None], proj[None], gain)


def solution(mesh):
    sections, plane = mesh.devices.shape
    core = 2
    side = math.isqrt(plane // core)
    fine = Mesh(mesh.devices.reshape(sections, side, side, core), ("section", *PLANE))
    placed = (
        P("section", PLANE, None, None, None),
        P(PLANE, None, None, None),
        P("section", None, None),
        P("section", None),
        P(PLANE, None),
    )
    return jax.shard_map(
        per_device,
        mesh=fine,
        in_specs=placed,
        out_specs=(
            P("section", PLANE, None, None, None),
            P("section", PLANE, None),
            P("section", PLANE),
        ),
        check_vma=False,
    )
```
